256 devices in a mesh: ctx: 32 (over y, z), tp: 8 (over x, core).
Axes of the slice: x: 4, y: 4, z: 8, core: 2. Of those that a mesh axis runs over, the one named last changes fastest.
Arguments:
- streams: bfloat16 [3, 4096, 8192], P(None, 'ctx', 'tp'), may hold values from -6 to 6
- short_filter: float32 [3, 7, 512], P(None, None, 'tp'), may hold values from -2.5 to 2.5
- residues: float32 [16, 512], P(None, 'tp'), may hold values from -0.125 to 0.125
- rates: float32 [16, 512], P(None, 'tp'), may hold values from 2.4414062e-06 to 0.04
- skip: float32 [8192], P('tp'), may hold values from 0.5 to 1.5
- out_weight: bfloat16 [4096, 8192], P('ctx', 'tp'), may hold values from -0.0625 to 0.0625
- out_cotangent: bfloat16 [4096, 4096], P('ctx', 'tp'), may hold values from -12 to 12
Outputs:
- output: bfloat16 [4096, 4096], P('ctx', 'tp')
- grad_streams: bfloat16 [3, 4096, 8192], P(None, 'ctx', 'tp')
- grad_short: float32 [3, 7, 512], P(None, None, 'tp')
- grad_skip: float32 [8192], P('tp')
- grad_weight: float32 [4096, 8192], P('ctx', 'tp')
The draws below stay inside these ranges and needn't reach their ends.
All inputs are finite; a program needn't handle non-finite values.
Results may differ from the reference program's by a relative error of at most 0.034.
Values may be sent and summed in bfloat16 or wider, within the bound.
A program may use at most 128 MiB of HBM per device.

```python
import math
import jax
import jax.numpy as jnp
from jax import lax

D = 8192
DOUT = 4096
MODES = 16
TAPS = 7
TOK_DEV = 128
GROUPS = 512
SEQ = 4096
N_TP = 8


def with_spikes(entries, rng, source, target, shards_of, factor):
    def block_of(position):
        return (jnp.arange(entries.shape[position]) // (entries.shape[position] // shards_of)).reshape((-1,) + (1,) * (entries.ndim - 1 - position))

    near = jax.random.permutation(rng, shards_of)[block_of(target)]
    other_side = (block_of(target) + shards_of // 2) % shards_of
    return jnp.where((block_of(source) == near) | (block_of(source) == other_side), factor * entries, entries)


def levels(key, dims, shards, least, top_value):
    def one(axis_at, parts):
        steps = jax.random.uniform(jax.random.fold_in(jax.random.fold_in(key, 6), axis_at), (parts,), jnp.float32, least / len(shards), top_value / len(shards))
        return jnp.repeat(jnp.exp(steps), dims[axis_at] // parts).reshape((-1,) + (1,) * (len(dims) - axis_at - 1))

    level = one(*shards[0])
    for cut in shards[1:]:
        level = level * one(*cut)
    return level


def normal_values(rng, extent, deviation, bound, cuts=(), kind=jnp.bfloat16):
    array = deviation * jax.random.normal(rng, extent, jnp.float32)
    if cuts:
        array = array * levels(rng, extent, cuts, -0.22, 0.18)
    return jnp.clip(array, -bound, bound).astype(kind)


def heavy_noise(stream_key, dims, spread, bound, cuts, heavy, held_as=jnp.bfloat16):
    drawn = spread * jax.random.normal(stream_key, dims, jnp.float32)
    if cuts:
        drawn = drawn * levels(stream_key, dims, cuts, -0.22, 0.18)
    return jnp.clip(with_spikes(drawn, jax.random.fold_in(stream_key, 3), *heavy), -bound, bound).astype(held_as)


def setup_inputs(seed: int = 0) -> dict:
    splits = jax.random.split(jax.random.key(seed), 8)
    streams = normal_values(splits[0], (3, SEQ, D), 1.0, 6.0, ((1, 32), (2, 8)))
    short_filter = normal_values(splits[1], (3, TAPS, GROUPS), 0.4, 2.5, ((2, 8),), jnp.float32)
    residues = normal_values(splits[2], (MODES, GROUPS), 0.02, 0.125, ((1, 8),), jnp.float32)
    rates = jnp.clip(jnp.exp(math.log(0.04) - 9.704061 * jax.random.uniform(splits[3], (MODES, GROUPS), jnp.float32) ** levels(splits[3], (MODES, GROUPS), ((1, 8),), -0.2, 0.2)), 2.441406195430318e-06, 0.04)
    skip = jnp.clip(0.5 + 1.0 * jax.random.uniform(splits[4], (D,), jnp.float32) ** levels(splits[4], (D,), ((0, 8),), -0.2, 0.2), 0.5, 1.5)
    out_weight = normal_values(splits[5], (DOUT, D), D ** -0.5, 0.0625, ((0, 32), (1, 8)))
    out_cotangent = heavy_noise(splits[6], (SEQ, DOUT), 1.0, 12.0, ((0, 32), (1, 8)), (0, 1, 32, 2.75))
    return {"streams": streams, "short_filter": short_filter, "residues": residues, "rates": rates, "skip": skip, "out_weight": out_weight, "out_cotangent": out_cotangent}


highest = lax.Precision.HIGHEST


def causal_modal(source, residues, rates):
    total_rows, channels = source.shape
    groups = residues.shape[1]
    members = channels // groups
    length = math.gcd(32, total_rows)
    positions = jnp.arange(length, dtype=jnp.float32)
    profile = jnp.sum(residues[:, None, :] * jnp.exp(-rates[:, None, :] * positions[None, :, None]), axis=0)
    counter = jnp.arange(length, dtype=jnp.int32)
    offset = counter[:, None] - counter[None, :]
    toeplitz = jnp.where((offset >= 0)[:, :, None], jnp.take(profile, jnp.maximum(offset, 0).astype(jnp.int32), axis=0), jnp.float32(0.0))
    inflow = jnp.exp(-rates[None] * (length - 1.0 - positions)[:, None, None])
    carried = residues[None] * jnp.exp(-rates[None] * (positions + 1.0)[:, None, None])
    decay = jnp.exp(-rates * length)
    blocks = source.reshape(total_rows // length, length, groups, members)

    def advance(state, part):
        local = jnp.einsum("tsg,sgc->tgc", toeplitz, part, precision=highest)
        local = local + jnp.einsum("tmg,mgc->tgc", carried, state, precision=highest)
        state = decay[:, :, None] * state + jnp.einsum("smg,sgc->mgc", inflow, part, precision=highest)
        return state, local

    initial = jnp.zeros((residues.shape[0], groups, members), dtype=jnp.float32)
    _, pieces = lax.scan(advance, initial, blocks)
    return pieces.reshape(total_rows, channels)


def reference(streams, short_filter, residues, rates, skip, out_weight, out_cotangent):
    total_rows = streams.shape[1]
    channels = streams.shape[2]
    groups = residues.shape[1]
    members = channels // groups
    reach = short_filter.shape[1] - 1
    taps = jnp.repeat(short_filter, members, axis=2)
    padded = jnp.pad(streams, ((0, 0), (reach, 0), (0, 0)))
    smoothed = jnp.zeros(streams.shape, jnp.float32)
    for lag in range(reach + 1):
        smoothed = smoothed + taps[:, lag, None, :] * padded[:, reach - lag:reach - lag + total_rows, :].astype(jnp.float32)
    mixed = lax.optimization_barrier((smoothed[1] * smoothed[2]).astype(jnp.bfloat16)).astype(jnp.float32)
    field = causal_modal(mixed, residues, rates) + skip * mixed
    gated = (smoothed[0] * field).astype(jnp.bfloat16)
    block_channels = channels // N_TP
    output_sum = jnp.zeros((total_rows, out_weight.shape[0]), jnp.float32)
    for member in range(N_TP):
        first = member * block_channels
        term = jnp.dot(gated[:, first:first + block_channels], out_weight[:, first:first + block_channels].T, preferred_element_type=jnp.float32)
        output_sum = output_sum + lax.optimization_barrier(term.astype(jnp.bfloat16)).astype(jnp.float32)
    output = output_sum.astype(jnp.bfloat16)
    upstream = jnp.dot(out_cotangent, out_weight, preferred_element_type=jnp.float32)

    def accumulate(total, index):
        cot_rows = lax.dynamic_slice_in_dim(out_cotangent, (index * TOK_DEV).astype(jnp.int32), TOK_DEV, 0)
        gate_rows = lax.dynamic_slice_in_dim(gated, (index * TOK_DEV).astype(jnp.int32), TOK_DEV, 0)
        term = lax.dot_general(cot_rows, gate_rows, (((0,), (0,)), ((), ())), preferred_element_type=jnp.float32)
        return total + lax.optimization_barrier(term.astype(jnp.bfloat16)).astype(jnp.float32), None

    grad_weight, _ = lax.scan(accumulate, jnp.zeros(out_weight.shape, jnp.float32), jnp.arange(total_rows // TOK_DEV, dtype=jnp.int32))
    grad_field = upstream * smoothed[0]
    grad_skip = jnp.sum(grad_field * mixed, axis=0)
    grad_mixed = causal_modal(grad_field[::-1], residues, rates)[::-1] + skip * grad_field
    grad_smoothed = jnp.stack([upstream * field, grad_mixed * smoothed[2], grad_mixed * smoothed[1]])
    tap_rows = []
    for lag in range(reach + 1):
        product = grad_smoothed * padded[:, reach - lag:reach - lag + total_rows, :].astype(jnp.float32)
        tap_rows.append(jnp.sum(product.reshape(3, total_rows, groups, members), axis=(1, 3)))
    grad_short = jnp.stack(tap_rows, axis=1)
    padded_back = jnp.pad(grad_smoothed, ((0, 0), (0, reach), (0, 0)))
    grad_streams = jnp.zeros(streams.shape, jnp.float32)
    for lag in range(reach + 1):
        grad_streams = grad_streams + taps[:, lag, None, :] * padded_back[:, lag:lag + total_rows, :]
    return output, grad_streams.astype(jnp.bfloat16), grad_short, grad_skip, grad_weight
```

```python
import functools

import jax
import jax.numpy as jnp
from jax import lax
from jax.experimental import pallas as pl
from jax.experimental.pallas import tpu as pltpu
from jax.sharding import PartitionSpec as P

F32 = jnp.float32
BF16 = jnp.bfloat16
HIGHEST = lax.Precision.HIGHEST
MESH = pl.DeviceIdType.MESH
ROWS = 128
LANES = 128
MEMBERS = 16
MODES = 16
TAPS = 7
PER_TILE = LANES // MEMBERS


def iota(shape, dim):
    return lax.broadcasted_iota(jnp.int32, shape, dim)


def two_terms(value):
    high = value.astype(BF16)
    return high, (value - high.astype(F32)).astype(BF16)


def kernel(
    dims,
    s_ref,
    sf_ref,
    res_ref,
    rate_ref,
    skip_ref,
    w_ref,
    cot_ref,
    out_ref,
    gs_ref,
    gshort_ref,
    gskip_ref,
    gw_ref,
    xpad,
    rim_in,
    sm,
    mixed,
    field,
    gfb,
    gm,
    tf,
    tb,
    inf,
    inb,
    entf,
    entb,
    rate_ch,
    dec,
    vecs,
    taps,
    prof,
    st_out,
    stz,
    tot,
    ret_out,
    bef,
    wg,
    cotg,
    gg,
    upp,
    up_in,
    outp,
    out_in,
    gwp,
    gw_r,
    gw_l,
    gsp,
    tapsum,
    sml,
    smz,
    smy,
    rim_sem,
    cot_s,
    cot_r,
    wr_sem,
    wl_sem,
    stz_sem,
    tot_sem,
    bef_sem,
    g_sem,
    up_sem,
    out_s,
    out_r,
    gwr_sem,
    gwl_sem,
    grim_sem,
    smz_sem,
    smy_sem,
):
    NX, NY, NZ, NK = dims
    C = s_ref.shape[2]
    G = sf_ref.shape[2]
    OT = cot_ref.shape[1]
    OY = NZ * ROWS
    R = NZ // 2
    L = NZ - 1 - R
    c = lax.axis_index("ctx")
    p = lax.axis_index("tp")
    y, z = lax.div(c, NZ), lax.rem(c, NZ)
    x, k = lax.div(p, NK), lax.rem(p, NK)
    last = NY * NZ - 1

    def dev(yy, zz, xx=x, kk=k):
        return (yy * NZ + zz, xx * NK + kk)

    def plus(a, d, n):
        return lax.rem(a + d + n, n)

    def remote(src, dst, ssem, rsem, to):
        return pltpu.make_async_remote_copy(
            src_ref=src, dst_ref=dst, send_sem=ssem, recv_sem=rsem, device_id=to, device_id_type=MESH
        )

    def rows_of(block):
        return pl.ds(pl.multiple_of(block * ROWS, ROWS), ROWS)

    def lanes_of(tile, width=LANES):
        return pl.ds(pl.multiple_of(tile * width, width), width)

    def unless_self(pair, body):
        if pair == (0, 0):
            pl.when(x != y)(body)
        else:
            body()

    pairs = [(a, b) for a in range(NX) for b in range(NK)]

    barrier = pltpu.get_barrier_semaphore()

    def greet(to):
        pl.semaphore_signal(barrier, inc=1, device_id=to, device_id_type=MESH)

    for d in range(1, NZ):
        greet(dev(y, plus(z, d, NZ)))
    for d in range(1, NY):
        greet(dev(plus(y, d, NY), z))
    for pair in pairs:
        unless_self(pair, lambda: greet(dev(x, z, plus(x, pair[0], NX), plus(k, pair[1], NK))))
        unless_self(pair, lambda: greet(dev(plus(y, pair[0], NY), z, y, plus(k, pair[1], NK))))

    @pl.when(c > 0)
    def _():
        greet((c - 1, p))

    @pl.when(c < last)
    def _():
        greet((c + 1, p))

    peers = NZ - 1 + NY - 1 + 2 * (NX * NK - 1)
    peers = peers + jnp.where(x != y, 2, 0) + jnp.where(c > 0, 1, 0) + jnp.where(c < last, 1, 0)
    pl.semaphore_wait(barrier, peers)

    rim_copy = remote(
        s_ref.at[:, pl.ds(ROWS - 16, 16), :], rim_in, rim_sem.at[0], rim_sem.at[1], (lax.rem(c + 1, last + 1), p)
    )

    @pl.when(c < last)
    def _():
        rim_copy.start()

    right, left = dev(y, plus(z, 1, NZ)), dev(y, plus(z, -1, NZ))
    wg[rows_of(z), :] = w_ref[...]

    def w_right(step):
        block = wg.at[rows_of(plus(z, -step, NZ)), :]
        return remote(block, block, wr_sem.at[0, step], wr_sem.at[1, step], right)

    def w_left(step):
        block = wg.at[rows_of(plus(z, step, NZ)), :]
        return remote(block, block, wl_sem.at[0, step], wl_sem.at[1, step], left)

    def w_arrived(step):
        if step <= R:
            block = wg.at[rows_of(plus(z, -step, NZ)), :]
            remote(block, block, wr_sem.at[0, step - 1], wr_sem.at[1, step - 1], right).wait_recv()
        if step < R:
            w_right(step).start()
        if step <= L:
            block = wg.at[rows_of(plus(z, step, NZ)), :]
            remote(block, block, wl_sem.at[0, step - 1], wl_sem.at[1, step - 1], left).wait_recv()
        if step < L:
            w_left(step).start()

    w_right(0).start()
    if L > 0:
        w_left(0).start()

    def cot_copy(pair):
        return remote(
            cot_ref,
            cotg.at[rows_of(y), lanes_of(k, OT)],
            cot_s.at[pair[0], pair[1]],
            cot_r.at[y, k],
            dev(x, z, plus(x, pair[0], NX), plus(k, pair[1], NK)),
        )

    for pair in pairs:
        unless_self(pair, lambda: cot_copy(pair).start())

    @pl.when(x == y)
    def _():
        cotg[rows_of(y), lanes_of(k, OT)] = cot_ref[...]

    spread = (lax.div(iota((G, C), 1), MEMBERS) == iota((G, C), 0)).astype(F32)
    rate_ch[...] = jnp.dot(rate_ref[...], spread, precision=HIGHEST, preferred_element_type=F32)
    res_ch = jnp.dot(res_ref[...], spread, precision=HIGHEST, preferred_element_type=F32)
    for i in range(3):
        taps[i, pl.ds(0, TAPS), :] = jnp.dot(
            sf_ref[i], spread, precision=HIGHEST, preferred_element_type=F32
        )
    own_mode = lax.rem(iota((MODES, C), 1), MODES) == iota((MODES, C), 0)
    dec[...] = jnp.exp(-float(ROWS) * rate_ch[...])
    vecs[pl.ds(0, 1), :] = jnp.sum(jnp.where(own_mode, rate_ch[...], 0.0), axis=0, keepdims=True)
    vecs[pl.ds(1, 1), :] = jnp.sum(jnp.where(own_mode, res_ch, 0.0), axis=0, keepdims=True)

    eye = (iota((G, G), 0) == iota((G, G), 1)).astype(F32)
    turned = (((1,), (1,)), ((), ()))
    rate_t = lax.dot_general(eye, rate_ref[...], turned, precision=HIGHEST, preferred_element_type=F32)
    res_t = lax.dot_general(eye, res_ref[...], turned, precision=HIGHEST, preferred_element_type=F32)
    lag = iota((G, LANES), 1).astype(F32)
    ahead = jnp.zeros((G, LANES), F32)
    behind = jnp.zeros((G, LANES), F32)
    for m in range(MODES):
        ahead = ahead + res_t[:, m : m + 1] * jnp.exp(-rate_t[:, m : m + 1] * lag)
        behind = behind + res_t[:, m : m + 1] * jnp.exp(-rate_t[:, m : m + 1] * (ROWS - 1.0 - lag))
    prof[0] = ahead
    prof[1] = behind

    row_id, lane_id = iota((ROWS, LANES), 0), iota((ROWS, LANES), 1)
    lane_group = lax.div(lane_id, MEMBERS)

    def tables(j, carry):
        ls = lanes_of(j)
        rate = vecs[pl.ds(0, 1), ls]
        amp = vecs[pl.ds(1, 1), ls] * jnp.exp(-rate)
        place = row_id.astype(F32)
        early = jnp.exp(-rate * place)
        late = jnp.exp(-rate * (ROWS - 1.0 - place))
        for table, value in ((inf, late), (inb, early)):
            high, low = two_terms(jnp.transpose(value))
            table[j, pl.ds(0, ROWS), :] = high
            table[j, pl.ds(ROWS, ROWS), :] = low
        for table, value in ((entf, amp * early), (entb, amp * late)):
            high, low = two_terms(value)
            table[j, :, pl.ds(0, LANES)] = high
            table[j, :, pl.ds(LANES, LANES)] = low
            table[j, :, pl.ds(2 * LANES, LANES)] = high
        return carry

    def toeplitz(j, carry):
        for g in range(PER_TILE):
            one = prof[0, pl.ds(j * PER_TILE + g, 1), :]
            skew = pltpu.roll(
                jnp.broadcast_to(one, (ROWS, LANES)), 0, 1, stride=1, stride_axis=0
            )
            tb[j, :, pl.ds(g * LANES, LANES)] = jnp.where(lane_id >= row_id, skew, 0.0).astype(BF16)
            one = prof[1, pl.ds(j * PER_TILE + g, 1), :]
            skew = pltpu.roll(
                jnp.broadcast_to(one, (ROWS, LANES)), 1, 1, stride=1, stride_axis=0
            )
            tf[j, :, pl.ds(g * LANES, LANES)] = jnp.where(lane_id <= row_id, skew, 0.0).astype(BF16)
        return carry

    lax.fori_loop(0, NZ, tables, 0)

    for i in range(3):
        xpad[i, pl.ds(8, ROWS), :] = s_ref[i].astype(F32)

    @pl.when(c == 0)
    def _():
        rim_in[...] = jnp.zeros_like(rim_in)

    @pl.when(c > 0)
    def _():
        rim_copy.wait_recv()

    for i in range(3):
        xpad[i, pl.ds(0, 8), :] = rim_in[i].astype(F32)[8:16, :]

    def spread_groups(value):
        return jnp.concatenate(
            [jnp.where(lane_group == g, value, 0.0).astype(BF16) for g in range(PER_TILE)], axis=0
        )

    mode_block = lax.div(row_id, MODES) == lane_group

    def state_of(table, value):
        both = jnp.dot(table, value, preferred_element_type=F32)
        both = jnp.where(mode_block, both[:ROWS] + both[ROWS:], 0.0)
        total = both[:MODES]
        for g in range(1, PER_TILE):
            total = total + both[g * MODES : (g + 1) * MODES]
        return total

    def from_state(table, state):
        tall = jnp.where(mode_block, jnp.concatenate([state] * PER_TILE, axis=0), 0.0)
        high, low = two_terms(tall)
        return jnp.dot(
            table, jnp.concatenate([high, high, low], axis=0), preferred_element_type=F32
        )

    def states_out(way):
        stz[way, z] = st_out[way, z]
        for d in range(1, NZ):
            to = plus(z, d, NZ)
            remote(
                st_out.at[way, to], stz.at[way, z], stz_sem.at[way, 0, d], stz_sem.at[way, 1, d], dev(y, to)
            ).start()

    def states_row(way):
        for d in range(1, NZ):
            src = plus(z, -d, NZ)
            remote(
                st_out.at[way, src], stz.at[way, src], stz_sem.at[way, 0, d], stz_sem.at[way, 1, d], dev(y, src)
            ).wait_recv()
        factor = dec[:, lanes_of(z)]
        state = jnp.zeros((MODES, LANES), F32)
        for i in range(NZ):
            at = i if way == 0 else NZ - 1 - i
            ret_out[way, at] = state
            state = factor * state + stz[way, at]
        tot[way, y] = state
        for d in range(1, NY):
            to = plus(y, d, NY)
            remote(
                tot.at[way, y], tot.at[way, y], tot_sem.at[way, 0, d], tot_sem.at[way, 1, d], dev(to, z)
            ).start()

    def states_back(way):
        for d in range(1, NY):
            src = plus(y, -d, NY)
            remote(
                tot.at[way, src], tot.at[way, src], tot_sem.at[way, 0, d], tot_sem.at[way, 1, d], dev(src, z)
            ).wait_recv()
        factor = dec[:, lanes_of(z)]
        row_factor = jnp.exp(-float(ROWS * NZ) * rate_ch[:, lanes_of(z)])
        state = jnp.zeros((MODES, LANES), F32)
        for i in range(NY):
            at = i if way == 0 else NY - 1 - i
            counts = (at < y) if way == 0 else (at > y)
            state = jnp.where(counts, row_factor * state + tot[way, at], state)
        for i in range(NZ):
            at = i if way == 0 else NZ - 1 - i
            ret_out[way, at] = ret_out[way, at] + state
            state = state * factor
        bef[way, z] = ret_out[way, z]
        for d in range(1, NZ):
            to = plus(z, d, NZ)
            remote(
                ret_out.at[way, to], bef.at[way, z], bef_sem.at[way, 0, d], bef_sem.at[way, 1, d], dev(y, to)
            ).start()

    def states_in(way):
        for d in range(1, NZ):
            src = plus(z, -d, NZ)
            remote(
                ret_out.at[way, src], bef.at[way, src], bef_sem.at[way, 0, d], bef_sem.at[way, 1, d], dev(y, src)
            ).wait_recv()

    def smooth(j, carry):
        ls = lanes_of(j)
        for i in range(3):
            total = taps[i, pl.ds(0, 1), ls] * xpad[i, pl.ds(8, ROWS), ls]
            for n in range(1, TAPS):
                total = total + taps[i, pl.ds(n, 1), ls] * xpad[i, pl.ds(8 - n, ROWS), ls]
            sm[i, :, ls] = total
        value = (sm[1, :, ls] * sm[2, :, ls]).astype(BF16)
        mixed[:, ls] = value
        st_out[0, j] = state_of(inf[j], value)
        return carry

    lax.fori_loop(0, NZ, smooth, 0)
    states_out(0)
    if NZ > 1:
        w_arrived(1)
    lax.fori_loop(0, NZ, toeplitz, 0)

    def local_field(j, carry):
        ls = lanes_of(j)
        value = mixed[:, ls].astype(F32)
        field[:, ls] = skip_ref[:, ls] * value + jnp.dot(
            tf[j], spread_groups(value), preferred_element_type=F32
        )
        return carry

    states_row(0)
    lax.fori_loop(0, NZ, local_field, 0)
    states_back(0)
    if R >= 2:
        w_arrived(2)
    states_in(0)

    def gate(j, carry):
        ls = lanes_of(j)
        value = field[:, ls] + from_state(entf[j], bef[0, j])
        field[:, ls] = value
        gg[rows_of(y), ls] = (sm[0, :, ls] * value).astype(BF16)
        return carry

    lax.fori_loop(0, NZ, gate, 0)

    def g_copy(d):
        return remote(
            gg.at[rows_of(y), :], gg.at[rows_of(y), :], g_sem.at[0, d], g_sem.at[1, d], dev(plus(y, d, NY), z)
        )

    for d in range(1, NY):
        g_copy(d).start()

    for step in range(3, R + 1):
        w_arrived(step)
    for a in range(NY):
        for b in range(NK):

            def cot_wait():
                block = cotg.at[pl.ds(a * ROWS, ROWS), pl.ds(b * OT, OT)]
                remote(block, block, cot_s.at[0, 0], cot_r.at[a, b], dev(y, z)).wait_recv()

            pl.when(jnp.logical_not((x == y) & (y == a) & (k == b)))(cot_wait)

    WIDE = 256

    def up_part(j, carry):
        ls = lanes_of(j, WIDE)
        upp[:, ls] = jnp.dot(cotg[...], wg[:, ls], preferred_element_type=F32).astype(BF16)
        return carry

    lax.fori_loop(0, C // WIDE, up_part, 0)

    def up_copy(d):
        to = plus(y, d, NY)
        return remote(upp.at[rows_of(to), :], up_in.at[d], up_sem.at[0, d], up_sem.at[1, d], dev(to, z))

    for d in range(1, NY):
        up_copy(d).start()

    for d in range(1, NY):
        src = plus(y, -d, NY)
        block = gg.at[rows_of(src), :]
        remote(block, block, g_sem.at[0, d], g_sem.at[1, d], dev(src, z)).wait_recv()

    over_rows = (((0,), (0,)), ((), ()))

    def gw_part(i, carry):
        block = lax.rem(z + R + NZ - i, NZ)
        gwp[block] = lax.dot_general(
            cotg[:, lanes_of(block)], gg[...], over_rows, preferred_element_type=F32
        ).astype(BF16)
        return carry

    def gw_right(step):
        return remote(
            gwp.at[plus(z, R - step, NZ)], gw_r.at[step], gwr_sem.at[0, step], gwr_sem.at[1, step], right
        )

    def gw_left(step):
        return remote(
            gwp.at[plus(z, step - L, NZ)], gw_l.at[step], gwl_sem.at[0, step], gwl_sem.at[1, step], left
        )

    def gw_arrived(step):
        if step <= R:
            gw_right(step - 1).wait_recv()
        if step < R:
            at = plus(z, R - step, NZ)
            gwp[at] = (gwp[at].astype(F32) + gw_r[step - 1].astype(F32)).astype(BF16)
            gw_right(step).start()
        if step <= L:
            gw_left(step - 1).wait_recv()
        if step < L:
            at = plus(z, step - L, NZ)
            gwp[at] = (gwp[at].astype(F32) + gw_l[step - 1].astype(F32)).astype(BF16)
            gw_left(step).start()

    lax.fori_loop(0, NZ, gw_part, 0)
    gw_right(0).start()
    if L > 0:
        gw_left(0).start()

    def out_part(j, carry):
        ls = lanes_of(j, WIDE)
        outp[:, ls] = lax.dot_general(gg[...], wg[ls, :], turned, preferred_element_type=F32).astype(BF16)
        return carry

    lax.fori_loop(0, OY // WIDE, out_part, 0)

    def out_copy(pair):
        yy, kk = plus(y, pair[0], NY), plus(k, pair[1], NK)
        return remote(
            outp.at[rows_of(yy), lanes_of(kk, OT)],
            out_in.at[p],
            out_s.at[pair[0], pair[1]],
            out_r.at[x, k],
            dev(yy, z, y, kk),
        )

    for pair in pairs:
        unless_self(pair, lambda: out_copy(pair).start())

    @pl.when(x == y)
    def _():
        out_in[p] = outp[rows_of(y), lanes_of(k, OT)]

    for d in range(1, NY):
        up_copy(d).wait_recv()

    def grad_field(j, carry):
        ls = lanes_of(j)
        up = upp[rows_of(y), ls].astype(F32)
        for d in range(1, NY):
            up = up + up_in[d, :, ls].astype(F32)
        gf = up * sm[0, :, ls]
        gsp[0, pl.ds(0, ROWS), ls] = up * field[:, ls]
        gm[:, ls] = skip_ref[:, ls] * gf
        sml[pl.ds(24 + j, 1), :] = jnp.sum(gf * mixed[:, ls].astype(F32), axis=0, keepdims=True)
        value = gf.astype(BF16)
        gfb[:, ls] = value
        st_out[1, j] = state_of(inb[j], value)
        return carry

    lax.fori_loop(0, NZ, grad_field, 0)
    states_out(1)

    def local_grad(j, carry):
        ls = lanes_of(j)
        gm[:, ls] = gm[:, ls] + jnp.dot(
            tb[j], spread_groups(gfb[:, ls].astype(F32)), preferred_element_type=F32
        )
        return carry

    def tap_grad(i, j):
        ls = lanes_of(j)
        value = gsp[i, pl.ds(0, ROWS), ls]
        for n in range(TAPS):
            tapsum[pl.ds(i * TAPS + n, 1), ls] = jnp.sum(
                value * xpad[i, pl.ds(8 - n, ROWS), ls], axis=0, keepdims=True
            )

    lax.fori_loop(0, NZ, local_grad, 0)
    states_row(1)
    gw_arrived(1)

    def first_taps(j, carry):
        tap_grad(0, j)
        return carry

    states_back(1)
    lax.fori_loop(0, NZ, first_taps, 0)
    states_in(1)

    def grad_mixed(j, carry):
        ls = lanes_of(j)
        value = gm[:, ls] + from_state(entb[j], bef[1, j])
        gsp[1, pl.ds(0, ROWS), ls] = value * sm[2, :, ls]
        gsp[2, pl.ds(0, ROWS), ls] = value * sm[1, :, ls]
        return carry

    lax.fori_loop(0, NZ, grad_mixed, 0)

    grim_copy = remote(
        gsp.at[:, pl.ds(0, 8), :],
        gsp.at[:, pl.ds(ROWS, 8), :],
        grim_sem.at[0],
        grim_sem.at[1],
        (lax.rem(c + last, last + 1), p),
    )

    @pl.when(c > 0)
    def _():
        grim_copy.start()

    if R >= 2:
        gw_arrived(2)

    def other_taps(j, carry):
        tap_grad(1, j)
        tap_grad(2, j)
        return carry

    lax.fori_loop(0, NZ, other_taps, 0)
    tapsum[pl.ds(3 * TAPS, 3), :] = jnp.zeros((3, C), F32)
    gather_groups = (lax.div(iota((C, LANES), 0), MEMBERS) == iota((C, LANES), 1)).astype(F32)
    sml[pl.ds(0, 24), :] = jnp.dot(
        tapsum[...], gather_groups, precision=HIGHEST, preferred_element_type=F32
    )

    def small_z(d):
        return remote(sml, smz.at[d], smz_sem.at[0, d], smz_sem.at[1, d], dev(y, plus(z, d, NZ)))

    def small_y(d):
        return remote(smy.at[0], smy.at[d], smy_sem.at[0, d], smy_sem.at[1, d], dev(plus(y, d, NY), z))

    for d in range(1, NZ):
        small_z(d).start()

    @pl.when(c == last)
    def _():
        gsp[:, pl.ds(ROWS, 8), :] = jnp.zeros((3, 8, C), F32)

    @pl.when(c < last)
    def _():
        grim_copy.wait_recv()

    def streams_grad(j, carry):
        ls = lanes_of(j)
        for i in range(3):
            total = taps[i, pl.ds(0, 1), ls] * gsp[i, pl.ds(0, ROWS), ls]
            for n in range(1, TAPS):
                total = total + taps[i, pl.ds(n, 1), ls] * gsp[i, pl.ds(n, ROWS), ls]
            gs_ref[i, :, ls] = total.astype(BF16)
        return carry

    lax.fori_loop(0, NZ, streams_grad, 0)

    total = sml[...]
    for d in range(1, NZ):
        small_z(d).wait_recv()
        total = total + smz[d]
    smy[0] = total
    for d in range(1, NY):
        small_y(d).start()

    for step in range(3, R + 1):
        gw_arrived(step)
    mine = gwp[z].astype(F32) + gw_r[R - 1].astype(F32)
    if L > 0:
        mine = mine + gw_l[L - 1].astype(F32)
    gw_ref[...] = mine

    for a in range(NX):
        for b in range(NK):

            def out_wait():
                block = out_in.at[a * NK + b]
                remote(block, block, out_s.at[0, 0], out_r.at[a, b], dev(y, z)).wait_recv()

            pl.when(jnp.logical_not((x == y) & (x == a) & (k == b)))(out_wait)
    value = out_in[0].astype(F32)
    for n in range(1, NX * NK):
        value = value + out_in[n].astype(F32)
    out_ref[...] = value.astype(BF16)

    total = smy[0]
    for d in range(1, NY):
        small_y(d).wait_recv()
        total = total + smy[d]
    for i in range(3):
        gshort_ref[i] = total[i * TAPS : (i + 1) * TAPS, :G]
    for j in range(NZ):
        gskip_ref[:, pl.ds(j * LANES, LANES)] = total[24 + j : 25 + j, :]

    @pl.when(c < last)
    def _():
        rim_copy.wait_send()

    @pl.when(c > 0)
    def _():
        grim_copy.wait_send()

    for step in range(R):
        w_right(step).wait_send()
        gw_right(step).wait_send()
    for step in range(L):
        w_left(step).wait_send()
        gw_left(step).wait_send()
    for pair in pairs:
        unless_self(pair, lambda: cot_copy(pair).wait_send())
        unless_self(pair, lambda: out_copy(pair).wait_send())
    for d in range(1, NY):
        g_copy(d).wait_send()
        up_copy(d).wait_send()
        small_y(d).wait_send()
        for way in range(2):
            remote(tot.at[way, y], tot.at[way, y], tot_sem.at[way, 0, d], tot_sem.at[way, 1, d], right).wait_send()
    for d in range(1, NZ):
        small_z(d).wait_send()
        for way in range(2):
            for buf, sem in ((st_out, stz_sem), (ret_out, bef_sem)):
                block = buf.at[way, plus(z, d, NZ)]
                remote(block, block, sem.at[way, 0, d], sem.at[way, 1, d], right).wait_send()


def shards(dims, streams, short_filter, residues, rates, skip, out_weight, out_cotangent):
    NX, NY, NZ, NK = dims
    C = streams.shape[2]
    G = residues.shape[1]
    OT = out_cotangent.shape[1]
    OY = NZ * ROWS
    R = NZ // 2
    L = max(NZ - 1 - R, 1)
    vmem = pltpu.VMEM
    dma = pltpu.SemaphoreType.DMA
    whole = pl.BlockSpec(memory_space=pltpu.VMEM)
    scratch = [
        vmem((3, ROWS + 8, C), F32),
        vmem((3, 16, C), BF16),
        vmem((3, ROWS, C), F32),
        vmem((ROWS, C), BF16),
        vmem((ROWS, C), F32),
        vmem((ROWS, C), BF16),
        vmem((ROWS, C), F32),
        vmem((NZ, ROWS, PER_TILE * LANES), BF16),
        vmem((NZ, ROWS, PER_TILE * LANES), BF16),
        vmem((NZ, 2 * ROWS, LANES), BF16),
        vmem((NZ, 2 * ROWS, LANES), BF16),
        vmem((NZ, ROWS, 3 * LANES), BF16),
        vmem((NZ, ROWS, 3 * LANES), BF16),
        vmem((MODES, C), F32),
        vmem((MODES, C), F32),
        vmem((8, C), F32),
        vmem((3, 8, C), F32),
        vmem((2, G, LANES), F32),
        vmem((2, NZ, MODES, LANES), F32),
        vmem((2, NZ, MODES, LANES), F32),
        vmem((2, NY, MODES, LANES), F32),
        vmem((2, NZ, MODES, LANES), F32),
        vmem((2, NZ, MODES, LANES), F32),
        vmem((OY, C), BF16),
        vmem((NY * ROWS, OY), BF16),
        vmem((NY * ROWS, C), BF16),
        vmem((NY * ROWS, C), BF16),
        vmem((NY, ROWS, C), BF16),
        vmem((NY * ROWS, OY), BF16),
        vmem((NX * NK, ROWS, OT), BF16),
        vmem((NZ, ROWS, C), BF16),
        vmem((R, ROWS, C), BF16),
        vmem((L, ROWS, C), BF16),
        vmem((3, ROWS + 8, C), F32),
        vmem((24, C), F32),
        vmem((32, LANES), F32),
        vmem((NZ, 32, LANES), F32),
        vmem((NY, 32, LANES), F32),
        dma((2,)),
        dma((NX, NK)),
        dma((NY, NK)),
        dma((2, R)),
        dma((2, L)),
        dma((2, 2, NZ)),
        dma((2, 2, NY)),
        dma((2, 2, NZ)),
        dma((2, NY)),
        dma((2, NY)),
        dma((NY, NK)),
        dma((NX, NK)),
        dma((2, R)),
        dma((2, L)),
        dma((2,)),
        dma((2, NZ)),
        dma((2, NY)),
    ]
    output, grad_streams, grad_short, grad_skip, grad_weight = pl.pallas_call(
        functools.partial(kernel, dims),
        out_shape=(
            jax.ShapeDtypeStruct((ROWS, OT), BF16),
            jax.ShapeDtypeStruct(streams.shape, BF16),
            jax.ShapeDtypeStruct(short_filter.shape, F32),
            jax.ShapeDtypeStruct((1, C), F32),
            jax.ShapeDtypeStruct((ROWS, C), F32),
        ),
        in_specs=[whole] * 7,
        out_specs=(whole,) * 5,
        scratch_shapes=scratch,
        compiler_params=pltpu.CompilerParams(
            collective_id=0, has_side_effects=True, vmem_limit_bytes=56 * 1024 * 1024
        ),
        name="mixer",
    )(streams, short_filter, residues, rates, skip.reshape(1, C), out_weight, out_cotangent)
    return output, grad_streams, grad_short, grad_skip.reshape(C), grad_weight


def build(mesh, dims):
    return jax.shard_map(
        functools.partial(shards, dims),
        mesh=mesh,
        in_specs=(
            P(None, "ctx", "tp"),
            P(None, None, "tp"),
            P(None, "tp"),
            P(None, "tp"),
            P("tp"),
            P("ctx", "tp"),
            P("ctx", "tp"),
        ),
        out_specs=(
            P("ctx", "tp"),
            P(None, "ctx", "tp"),
            P(None, None, "tp"),
            P("tp"),
            P("ctx", "tp"),
        ),
        check_vma=False,
    )


def solution(mesh):
    return build(mesh, (4, 4, 8, 2))
```

```python
import functools

import jax
import jax.numpy as jnp
from jax import lax
from jax.experimental import pallas as pl
from jax.experimental.pallas import tpu as pltpu
from jax.sharding import PartitionSpec as P

F32 = jnp.float32
BF16 = jnp.bfloat16
HIGHEST = lax.Precision.HIGHEST
MESH = pl.DeviceIdType.MESH
ROWS = 128
HALF = 64
LANES = 128
MEMBERS = 16
MODES = 16
TAPS = 7
PER_TILE = LANES // MEMBERS


def iota(shape, dim):
    return lax.broadcasted_iota(jnp.int32, shape, dim)


def two_terms(value):
    high = value.astype(BF16)
    return high, (value - high.astype(F32)).astype(BF16)


def kernel(
    dims,
    s_ref,
    sf_ref,
    res_ref,
    rate_ref,
    skip_ref,
    w_ref,
    cot_ref,
    out_ref,
    gs_ref,
    gshort_ref,
    gskip_ref,
    gw_ref,
    xpad,
    rim_in,
    sm,
    mixed,
    field,
    gfb,
    gm,
    tf,
    tb,
    inf,
    inb,
    entf,
    entb,
    rate_ch,
    dec,
    vecs,
    taps,
    prof,
    st_out,
    stz,
    tot,
    ret_out,
    bef,
    wg,
    cotg,
    gg,
    upp,
    up_in,
    outp,
    pair_in,
    outh,
    out_y,
    out_x,
    gwp,
    gw_r,
    gw_l,
    gsp,
    tapsum,
    sml,
    smz,
    smy,
    rim_sem,
    cot_s,
    cot_r,
    wr_sem,
    wl_sem,
    stz_sem,
    tot_sem,
    bef_sem,
    g_sem,
    up_sem,
    pair_sem,
    outy_sem,
    outx_sem,
    gwr_sem,
    gwl_sem,
    grim_sem,
    smz_sem,
    smy_sem,
):
    NX, NY, NZ, NK = dims
    C = s_ref.shape[2]
    G = sf_ref.shape[2]
    OT = cot_ref.shape[1]
    OY = NZ * ROWS
    R = NZ // 2
    c = lax.axis_index("ctx")
    p = lax.axis_index("tp")
    y, z = lax.div(c, NZ), lax.rem(c, NZ)
    x, k = lax.div(p, NK), lax.rem(p, NK)
    last = NY * NZ - 1

    def dev(yy, zz, xx=x, kk=k):
        return (yy * NZ + zz, xx * NK + kk)

    def plus(a, d, n):
        return lax.rem(a + d + n, n)

    def remote(src, dst, ssem, rsem, to):
        return pltpu.make_async_remote_copy(
            src_ref=src, dst_ref=dst, send_sem=ssem, recv_sem=rsem, device_id=to, device_id_type=MESH
        )

    def rows_of(block):
        return pl.ds(pl.multiple_of(block * ROWS, ROWS), ROWS)

    def lanes_of(tile, width=LANES):
        return pl.ds(pl.multiple_of(tile * width, width), width)

    def unless_self(pair, body):
        if pair == (0, 0):
            pl.when(x != y)(body)
        else:
            body()

    pairs = [(a, b) for a in range(NX) for b in range(NK)]

    barrier = pltpu.get_barrier_semaphore()

    def greet(to):
        pl.semaphore_signal(barrier, inc=1, device_id=to, device_id_type=MESH)

    for d in range(1, NZ):
        greet(dev(y, plus(z, d, NZ)))
    for d in range(1, NY):
        greet(dev(plus(y, d, NY), z))
    for d in range(1, NX):
        greet(dev(y, z, plus(x, d, NX)))
    for d in range(1, NK):
        greet(dev(y, z, x, plus(k, d, NK)))
    for pair in pairs:
        unless_self(pair, lambda: greet(dev(x, z, plus(x, pair[0], NX), plus(k, pair[1], NK))))
        unless_self(pair, lambda: greet(dev(plus(y, pair[0], NY), z, y, plus(k, pair[1], NK))))

    @pl.when(c > 0)
    def _():
        greet((c - 1, p))

    @pl.when(c < last)
    def _():
        greet((c + 1, p))

    spread = (lax.div(iota((G, C), 1), MEMBERS) == iota((G, C), 0)).astype(F32)
    rate_ch[...] = jnp.dot(rate_ref[...], spread, precision=HIGHEST, preferred_element_type=F32)
    res_ch = jnp.dot(res_ref[...], spread, precision=HIGHEST, preferred_element_type=F32)
    for i in range(3):
        taps[i, pl.ds(0, TAPS), :] = jnp.dot(
            sf_ref[i], spread, precision=HIGHEST, preferred_element_type=F32
        )
    own_mode = lax.rem(iota((MODES, C), 1), MODES) == iota((MODES, C), 0)
    dec[...] = jnp.exp(-float(ROWS) * rate_ch[...])
    vecs[pl.ds(0, 1), :] = jnp.sum(jnp.where(own_mode, rate_ch[...], 0.0), axis=0, keepdims=True)
    vecs[pl.ds(1, 1), :] = jnp.sum(jnp.where(own_mode, res_ch, 0.0), axis=0, keepdims=True)

    eye = (iota((G, G), 0) == iota((G, G), 1)).astype(F32)
    turned = (((1,), (1,)), ((), ()))
    rate_t = lax.dot_general(eye, rate_ref[...], turned, precision=HIGHEST, preferred_element_type=F32)
    res_t = lax.dot_general(eye, res_ref[...], turned, precision=HIGHEST, preferred_element_type=F32)
    lag = iota((G, LANES), 1).astype(F32)
    ahead = jnp.zeros((G, LANES), F32)
    behind = jnp.zeros((G, LANES), F32)
    for m in range(MODES):
        ahead = ahead + res_t[:, m : m + 1] * jnp.exp(-rate_t[:, m : m + 1] * lag)
        behind = behind + res_t[:, m : m + 1] * jnp.exp(-rate_t[:, m : m + 1] * (ROWS - 1.0 - lag))
    prof[0] = ahead
    prof[1] = behind

    row_id, lane_id = iota((ROWS, LANES), 0), iota((ROWS, LANES), 1)
    lane_group = lax.div(lane_id, MEMBERS)

    def tables(j, carry):
        ls = lanes_of(j)
        rate = vecs[pl.ds(0, 1), ls]
        amp = vecs[pl.ds(1, 1), ls] * jnp.exp(-rate)
        place = row_id.astype(F32)
        early = jnp.exp(-rate * place)
        late = jnp.exp(-rate * (ROWS - 1.0 - place))
        for table, value in ((inf, late), (inb, early)):
            high, low = two_terms(jnp.transpose(value))
            table[j, pl.ds(0, ROWS), :] = high
            table[j, pl.ds(ROWS, ROWS), :] = low
        for table, value in ((entf, amp * early), (entb, amp * late)):
            high, low = two_terms(value)
            table[j, :, pl.ds(0, LANES)] = high
            table[j, :, pl.ds(LANES, LANES)] = low
            table[j, :, pl.ds(2 * LANES, LANES)] = high
        return carry

    def toeplitz(j, carry):
        for g in range(PER_TILE):
            one = prof[0, pl.ds(j * PER_TILE + g, 1), :]
            skew = pltpu.roll(
                jnp.broadcast_to(one, (ROWS, LANES)), 0, 1, stride=1, stride_axis=0
            )
            tb[j, :, pl.ds(g * LANES, LANES)] = jnp.where(lane_id >= row_id, skew, 0.0).astype(BF16)
            one = prof[1, pl.ds(j * PER_TILE + g, 1), :]
            skew = pltpu.roll(
                jnp.broadcast_to(one, (ROWS, LANES)), 1, 1, stride=1, stride_axis=0
            )
            tf[j, :, pl.ds(g * LANES, LANES)] = jnp.where(lane_id <= row_id, skew, 0.0).astype(BF16)
        return carry

    lax.fori_loop(0, NZ, tables, 0)

    for i in range(3):
        xpad[i, pl.ds(8, ROWS), :] = s_ref[i].astype(F32)

    peers = NZ - 1 + NY - 1 + NX - 1 + NK - 1 + 2 * (NX * NK - 1)
    peers = peers + jnp.where(x != y, 2, 0) + jnp.where(c > 0, 1, 0) + jnp.where(c < last, 1, 0)
    pl.semaphore_wait(barrier, peers)

    rim_copy = remote(
        s_ref.at[:, pl.ds(ROWS - 16, 16), :], rim_in, rim_sem.at[0], rim_sem.at[1], (lax.rem(c + 1, last + 1), p)
    )

    @pl.when(c < last)
    def _():
        rim_copy.start()

    right, left = dev(y, plus(z, 1, NZ)), dev(y, plus(z, -1, NZ))
    wg[rows_of(z), :] = w_ref[...]

    def long_way(direction, half):
        return R if direction == half else R - 1

    def half_rows(block, half):
        return pl.ds(pl.multiple_of(block * ROWS + half * HALF, HALF), HALF)

    def w_copy(direction, half, step):
        sem = wr_sem if direction == 0 else wl_sem
        block = wg.at[half_rows(plus(z, -step if direction == 0 else step, NZ), half), :]
        return remote(block, block, sem.at[0, half, step], sem.at[1, half, step], right if direction == 0 else left)

    def w_arrived(step, lap):
        for direction in range(2):
            half = direction if lap == 0 else 1 - direction
            steps = long_way(direction, half)
            if step <= steps:
                sem = wr_sem if direction == 0 else wl_sem
                block = wg.at[half_rows(plus(z, -step if direction == 0 else step, NZ), half), :]
                remote(block, block, sem.at[0, half, step - 1], sem.at[1, half, step - 1], right).wait_recv()
            if step < steps:
                w_copy(direction, half, step).start()

    for lap in range(2):
        for direction in range(2):
            half = direction if lap == 0 else 1 - direction
            if long_way(direction, half) > 0:
                w_copy(direction, half, 0).start()

    def cot_copy(pair):
        return remote(
            cot_ref,
            cotg.at[rows_of(y), lanes_of(k, OT)],
            cot_s.at[pair[0], pair[1]],
            cot_r.at[y, k],
            dev(x, z, plus(x, pair[0], NX), plus(k, pair[1], NK)),
        )

    for pair in pairs:
        unless_self(pair, lambda: cot_copy(pair).start())

    @pl.when(x == y)
    def _():
        cotg[rows_of(y), lanes_of(k, OT)] = cot_ref[...]

    lax.fori_loop(0, NZ, toeplitz, 0)

    @pl.when(c == 0)
    def _():
        rim_in[...] = jnp.zeros_like(rim_in)

    @pl.when(c > 0)
    def _():
        rim_copy.wait_recv()

    for i in range(3):
        xpad[i, pl.ds(0, 8), :] = rim_in[i].astype(F32)[8:16, :]

    def spread_groups(value):
        return jnp.concatenate(
            [jnp.where(lane_group == g, value, 0.0).astype(BF16) for g in range(PER_TILE)], axis=0
        )

    mode_block = lax.div(row_id, MODES) == lane_group

    def state_of(table, value):
        both = jnp.dot(table, value, preferred_element_type=F32)
        both = jnp.where(mode_block, both[:ROWS] + both[ROWS:], 0.0)
        total = both[:MODES]
        for g in range(1, PER_TILE):
            total = total + both[g * MODES : (g + 1) * MODES]
        return total

    def from_state(table, state):
        tall = jnp.where(mode_block, jnp.concatenate([state] * PER_TILE, axis=0), 0.0)
        high, low = two_terms(tall)
        return jnp.dot(
            table, jnp.concatenate([high, high, low], axis=0), preferred_element_type=F32
        )

    def states_out(way):
        stz[way, z] = st_out[way, z]
        for d in range(1, NZ):
            to = plus(z, d, NZ)
            remote(
                st_out.at[way, to], stz.at[way, z], stz_sem.at[way, 0, d], stz_sem.at[way, 1, d], dev(y, to)
            ).start()

    def states_row(way):
        for d in range(1, NZ):
            src = plus(z, -d, NZ)
            remote(
                st_out.at[way, src], stz.at[way, src], stz_sem.at[way, 0, d], stz_sem.at[way, 1, d], dev(y, src)
            ).wait_recv()
        factor = dec[:, lanes_of(z)]
        state = jnp.zeros((MODES, LANES), F32)
        for i in range(NZ):
            at = i if way == 0 else NZ - 1 - i
            ret_out[way, at] = state
            state = factor * state + stz[way, at]
        tot[way, y] = state
        for d in range(1, NY):
            to = plus(y, d, NY)
            remote(
                tot.at[way, y], tot.at[way, y], tot_sem.at[way, 0, d], tot_sem.at[way, 1, d], dev(to, z)
            ).start()

    def states_back(way):
        for d in range(1, NY):
            src = plus(y, -d, NY)
            remote(
                tot.at[way, src], tot.at[way, src], tot_sem.at[way, 0, d], tot_sem.at[way, 1, d], dev(src, z)
            ).wait_recv()
        factor = dec[:, lanes_of(z)]
        row_factor = jnp.exp(-float(ROWS * NZ) * rate_ch[:, lanes_of(z)])
        state = jnp.zeros((MODES, LANES), F32)
        for i in range(NY):
            at = i if way == 0 else NY - 1 - i
            counts = (at < y) if way == 0 else (at > y)
            state = jnp.where(counts, row_factor * state + tot[way, at], state)
        for i in range(NZ):
            at = i if way == 0 else NZ - 1 - i
            ret_out[way, at] = ret_out[way, at] + state
            state = state * factor
        bef[way, z] = ret_out[way, z]
        for d in range(1, NZ):
            to = plus(z, d, NZ)
            remote(
                ret_out.at[way, to], bef.at[way, z], bef_sem.at[way, 0, d], bef_sem.at[way, 1, d], dev(y, to)
            ).start()

    def states_in(way):
        for d in range(1, NZ):
            src = plus(z, -d, NZ)
            remote(
                ret_out.at[way, src], bef.at[way, src], bef_sem.at[way, 0, d], bef_sem.at[way, 1, d], dev(y, src)
            ).wait_recv()

    def smooth(j, carry):
        ls = lanes_of(j)
        for i in range(3):
            total = taps[i, pl.ds(0, 1), ls] * xpad[i, pl.ds(8, ROWS), ls]
            for n in range(1, TAPS):
                total = total + taps[i, pl.ds(n, 1), ls] * xpad[i, pl.ds(8 - n, ROWS), ls]
            sm[i, :, ls] = total
        value = (sm[1, :, ls] * sm[2, :, ls]).astype(BF16)
        mixed[:, ls] = value
        st_out[0, j] = state_of(inf[j], value)
        return carry

    lax.fori_loop(0, NZ, smooth, 0)
    states_out(0)
    w_arrived(1, 0)

    def local_field(j, carry):
        ls = lanes_of(j)
        value = mixed[:, ls].astype(F32)
        field[:, ls] = skip_ref[:, ls] * value + jnp.dot(
            tf[j], spread_groups(value), preferred_element_type=F32
        )
        return carry

    lax.fori_loop(0, R, local_field, 0)
    w_arrived(1, 1)
    lax.fori_loop(R, NZ, local_field, 0)
    for step, lap in [(2, 0)]:
        w_arrived(step, lap)
    states_row(0)
    for step, lap in [(2, 1), (3, 0)]:
        w_arrived(step, lap)
    states_back(0)
    for step, lap in [(3, 1)] + [(n, lap) for n in range(4, R + 1) for lap in range(2)]:
        w_arrived(step, lap)
    states_in(0)

    def gate(j, carry):
        ls = lanes_of(j)
        value = field[:, ls] + from_state(entf[j], bef[0, j])
        field[:, ls] = value
        gg[rows_of(y), ls] = (sm[0, :, ls] * value).astype(BF16)
        return carry

    lax.fori_loop(0, NZ, gate, 0)

    def g_copy(d):
        return remote(
            gg.at[rows_of(y), :], gg.at[rows_of(y), :], g_sem.at[0, d], g_sem.at[1, d], dev(plus(y, d, NY), z)
        )

    for d in range(1, NY):
        g_copy(d).start()

    for a in range(NY):
        for b in range(NK):

            def cot_wait():
                block = cotg.at[pl.ds(a * ROWS, ROWS), pl.ds(b * OT, OT)]
                remote(block, block, cot_s.at[0, 0], cot_r.at[a, b], dev(y, z)).wait_recv()

            pl.when(jnp.logical_not((x == y) & (y == a) & (k == b)))(cot_wait)

    WIDE = 256

    def up_part(j, carry):
        ls = lanes_of(j, WIDE)
        upp[:, ls] = jnp.dot(cotg[...], wg[:, ls], preferred_element_type=F32).astype(BF16)
        return carry

    lax.fori_loop(0, C // WIDE, up_part, 0)

    def up_copy(d):
        to = plus(y, d, NY)
        return remote(upp.at[rows_of(to), :], up_in.at[d], up_sem.at[0, d], up_sem.at[1, d], dev(to, z))

    for d in range(1, NY):
        up_copy(d).start()

    for d in range(1, NY):
        src = plus(y, -d, NY)
        block = gg.at[rows_of(src), :]
        remote(block, block, g_sem.at[0, d], g_sem.at[1, d], dev(src, z)).wait_recv()

    over_rows = (((0,), (0,)), ((), ()))

    def gw_part(i, carry):
        block = lax.rem(z + R + NZ - i, NZ)
        gwp[block] = lax.dot_general(
            cotg[:, lanes_of(block)], gg[...], over_rows, preferred_element_type=F32
        ).astype(BF16)
        return carry

    def gw_block(direction, half, step):
        far = long_way(direction, half) - step
        return plus(z, far if direction == 0 else -far, NZ)

    def gw_copy(direction, half, step):
        sem, into = (gwr_sem, gw_r) if direction == 0 else (gwl_sem, gw_l)
        return remote(
            gwp.at[gw_block(direction, half, step), pl.ds(half * HALF, HALF), :],
            into.at[half, step],
            sem.at[0, half, step],
            sem.at[1, half, step],
            right if direction == 0 else left,
        )

    def gw_arrived(step, lap):
        for direction in range(2):
            half = direction if lap == 0 else 1 - direction
            steps = long_way(direction, half)
            if step <= steps:
                gw_copy(direction, half, step - 1).wait_recv()
            if step < steps:
                at = gw_block(direction, half, step)
                came = gw_r if direction == 0 else gw_l
                rows = pl.ds(half * HALF, HALF)
                gwp[at, rows, :] = (gwp[at, rows, :].astype(F32) + came[half, step - 1].astype(F32)).astype(BF16)
                gw_copy(direction, half, step).start()

    lax.fori_loop(0, NZ, gw_part, 0)
    for lap in range(2):
        for direction in range(2):
            half = direction if lap == 0 else 1 - direction
            if long_way(direction, half) > 0:
                gw_copy(direction, half, 0).start()

    def out_part(j, carry):
        ls = lanes_of(j, WIDE)
        outp[:, ls] = lax.dot_general(gg[...], wg[ls, :], turned, preferred_element_type=F32).astype(BF16)
        return carry

    lax.fori_loop(0, OY // WIDE, out_part, 0)

    def pair_copy():
        return remote(
            outp.at[:, lanes_of(1 - k, OT)], pair_in, pair_sem.at[0], pair_sem.at[1], dev(y, z, x, 1 - k)
        )

    def outy_copy(d):
        to = plus(y, d, NY)
        return remote(outh.at[rows_of(to), :], out_y.at[y], outy_sem.at[0, d], outy_sem.at[1, d], dev(to, z))

    def outx_copy(d):
        to = plus(x, d, NX)
        return remote(out_y.at[to], out_x.at[x], outx_sem.at[0, d], outx_sem.at[1, d], dev(y, z, to))

    if NK == 2:
        pair_copy().start()

    def out_over_y():
        if NK == 2:
            pair_copy().wait_recv()
            outh[...] = (outp[:, lanes_of(k, OT)].astype(F32) + pair_in[...].astype(F32)).astype(BF16)
        else:
            outh[...] = outp[...]
        for d in range(1, NY):
            outy_copy(d).start()
        out_y[y] = outh[rows_of(y), :]

    def out_over_x():
        for d in range(1, NY):
            block = out_y.at[plus(y, -d, NY)]
            remote(block, block, outy_sem.at[0, d], outy_sem.at[1, d], right).wait_recv()
        for d in range(1, NX):
            outx_copy(d).start()
        out_x[x] = out_y[x]

    def out_done():
        for d in range(1, NX):
            block = out_x.at[plus(x, -d, NX)]
            remote(block, block, outx_sem.at[0, d], outx_sem.at[1, d], right).wait_recv()
        value = out_x[0].astype(F32)
        for n in range(1, NX):
            value = value + out_x[n].astype(F32)
        out_ref[...] = value.astype(BF16)

    gw_arrived(1, 0)
    out_over_y()
    gw_arrived(1, 1)

    for d in range(1, NY):
        up_copy(d).wait_recv()

    def grad_field(j, carry):
        ls = lanes_of(j)
        up = upp[rows_of(y), ls].astype(F32)
        for d in range(1, NY):
            up = up + up_in[d, :, ls].astype(F32)
        gf = up * sm[0, :, ls]
        gsp[0, pl.ds(0, ROWS), ls] = up * field[:, ls]
        gm[:, ls] = skip_ref[:, ls] * gf
        sml[pl.ds(24 + j, 1), :] = jnp.sum(gf * mixed[:, ls].astype(F32), axis=0, keepdims=True)
        value = gf.astype(BF16)
        gfb[:, ls] = value
        st_out[1, j] = state_of(inb[j], value)
        return carry

    lax.fori_loop(0, NZ, grad_field, 0)
    states_out(1)

    def local_grad(j, carry):
        ls = lanes_of(j)
        gm[:, ls] = gm[:, ls] + jnp.dot(
            tb[j], spread_groups(gfb[:, ls].astype(F32)), preferred_element_type=F32
        )
        return carry

    def tap_grad(i, j):
        ls = lanes_of(j)
        value = gsp[i, pl.ds(0, ROWS), ls]
        for n in range(TAPS):
            tapsum[pl.ds(i * TAPS + n, 1), ls] = jnp.sum(
                value * xpad[i, pl.ds(8 - n, ROWS), ls], axis=0, keepdims=True
            )

    gw_arrived(2, 0)
    lax.fori_loop(0, NZ, local_grad, 0)
    gw_arrived(2, 1)
    out_over_x()
    states_row(1)
    gw_arrived(3, 0)

    def first_taps(j, carry):
        tap_grad(0, j)
        return carry

    lax.fori_loop(0, NZ, first_taps, 0)
    states_back(1)
    gw_arrived(3, 1)
    out_done()
    for n in range(4, R + 1):
        for lap in range(2):
            gw_arrived(n, lap)
    for half in range(2):
        rows = pl.ds(half * HALF, HALF)
        mine = gwp[z, rows, :].astype(F32)
        for direction, came in ((0, gw_r), (1, gw_l)):
            if long_way(direction, half) > 0:
                mine = mine + came[half, long_way(direction, half) - 1].astype(F32)
        gw_ref[rows, :] = mine
    states_in(1)

    def grad_mixed(j, carry):
        ls = lanes_of(j)
        value = gm[:, ls] + from_state(entb[j], bef[1, j])
        gsp[1, pl.ds(0, ROWS), ls] = value * sm[2, :, ls]
        gsp[2, pl.ds(0, ROWS), ls] = value * sm[1, :, ls]
        return carry

    lax.fori_loop(0, NZ, grad_mixed, 0)

    grim_copy = remote(
        gsp.at[:, pl.ds(0, 8), :],
        gsp.at[:, pl.ds(ROWS, 8), :],
        grim_sem.at[0],
        grim_sem.at[1],
        (lax.rem(c + last, last + 1), p),
    )

    @pl.when(c > 0)
    def _():
        grim_copy.start()

    def other_taps(j, carry):
        tap_grad(1, j)
        tap_grad(2, j)
        return carry

    lax.fori_loop(0, NZ, other_taps, 0)
    tapsum[pl.ds(3 * TAPS, 3), :] = jnp.zeros((3, C), F32)
    gather_groups = (lax.div(iota((C, LANES), 0), MEMBERS) == iota((C, LANES), 1)).astype(F32)
    sml[pl.ds(0, 24), :] = jnp.dot(
        tapsum[...], gather_groups, precision=HIGHEST, preferred_element_type=F32
    )

    def small_z(d):
        return remote(sml, smz.at[d], smz_sem.at[0, d], smz_sem.at[1, d], dev(y, plus(z, d, NZ)))

    def small_y(d):
        return remote(smy.at[0], smy.at[d], smy_sem.at[0, d], smy_sem.at[1, d], dev(plus(y, d, NY), z))

    for d in range(1, NZ):
        small_z(d).start()

    @pl.when(c == last)
    def _():
        gsp[:, pl.ds(ROWS, 8), :] = jnp.zeros((3, 8, C), F32)

    @pl.when(c < last)
    def _():
        grim_copy.wait_recv()

    def streams_grad(j, carry):
        ls = lanes_of(j)
        for i in range(3):
            total = taps[i, pl.ds(0, 1), ls] * gsp[i, pl.ds(0, ROWS), ls]
            for n in range(1, TAPS):
                total = total + taps[i, pl.ds(n, 1), ls] * gsp[i, pl.ds(n, ROWS), ls]
            gs_ref[i, :, ls] = total.astype(BF16)
        return carry

    lax.fori_loop(0, NZ, streams_grad, 0)

    total = sml[...]
    for d in range(1, NZ):
        small_z(d).wait_recv()
        total = total + smz[d]
    smy[0] = total
    for d in range(1, NY):
        small_y(d).start()

    total = smy[0]
    for d in range(1, NY):
        small_y(d).wait_recv()
        total = total + smy[d]
    for i in range(3):
        gshort_ref[i] = total[i * TAPS : (i + 1) * TAPS, :G]
    for j in range(NZ):
        gskip_ref[:, pl.ds(j * LANES, LANES)] = total[24 + j : 25 + j, :]

    @pl.when(c < last)
    def _():
        rim_copy.wait_send()

    @pl.when(c > 0)
    def _():
        grim_copy.wait_send()

    for direction in range(2):
        for half in range(2):
            for step in range(long_way(direction, half)):
                w_copy(direction, half, step).wait_send()
                gw_copy(direction, half, step).wait_send()
    for pair in pairs:
        unless_self(pair, lambda: cot_copy(pair).wait_send())
    if NK == 2:
        pair_copy().wait_send()
    for d in range(1, NX):
        outx_copy(d).wait_send()
    for d in range(1, NY):
        outy_copy(d).wait_send()
    for d in range(1, NY):
        g_copy(d).wait_send()
        up_copy(d).wait_send()
        small_y(d).wait_send()
        for way in range(2):
            remote(tot.at[way, y], tot.at[way, y], tot_sem.at[way, 0, d], tot_sem.at[way, 1, d], right).wait_send()
    for d in range(1, NZ):
        small_z(d).wait_send()
        for way in range(2):
            for buf, sem in ((st_out, stz_sem), (ret_out, bef_sem)):
                block = buf.at[way, plus(z, d, NZ)]
                remote(block, block, sem.at[way, 0, d], sem.at[way, 1, d], right).wait_send()


def shards(dims, streams, short_filter, residues, rates, skip, out_weight, out_cotangent):
    NX, NY, NZ, NK = dims
    C = streams.shape[2]
    G = residues.shape[1]
    OT = out_cotangent.shape[1]
    OY = NZ * ROWS
    R = NZ // 2
    vmem = pltpu.VMEM
    dma = pltpu.SemaphoreType.DMA
    whole = pl.BlockSpec(memory_space=pltpu.VMEM)
    scratch = [
        vmem((3, ROWS + 8, C), F32),
        vmem((3, 16, C), BF16),
        vmem((3, ROWS, C), F32),
        vmem((ROWS, C), BF16),
        vmem((ROWS, C), F32),
        vmem((ROWS, C), BF16),
        vmem((ROWS, C), F32),
        vmem((NZ, ROWS, PER_TILE * LANES), BF16),
        vmem((NZ, ROWS, PER_TILE * LANES), BF16),
        vmem((NZ, 2 * ROWS, LANES), BF16),
        vmem((NZ, 2 * ROWS, LANES), BF16),
        vmem((NZ, ROWS, 3 * LANES), BF16),
        vmem((NZ, ROWS, 3 * LANES), BF16),
        vmem((MODES, C), F32),
        vmem((MODES, C), F32),
        vmem((8, C), F32),
        vmem((3, 8, C), F32),
        vmem((2, G, LANES), F32),
        vmem((2, NZ, MODES, LANES), F32),
        vmem((2, NZ, MODES, LANES), F32),
        vmem((2, NY, MODES, LANES), F32),
        vmem((2, NZ, MODES, LANES), F32),
        vmem((2, NZ, MODES, LANES), F32),
        vmem((OY, C), BF16),
        vmem((NY * ROWS, OY), BF16),
        vmem((NY * ROWS, C), BF16),
        vmem((NY * ROWS, C), BF16),
        vmem((NY, ROWS, C), BF16),
        vmem((NY * ROWS, OY), BF16),
        vmem((NY * ROWS, OT), BF16),
        vmem((NY * ROWS, OT), BF16),
        vmem((NY, ROWS, OT), BF16),
        vmem((NX, ROWS, OT), BF16),
        vmem((NZ, ROWS, C), BF16),
        vmem((2, R, HALF, C), BF16),
        vmem((2, R, HALF, C), BF16),
        vmem((3, ROWS + 8, C), F32),
        vmem((24, C), F32),
        vmem((32, LANES), F32),
        vmem((NZ, 32, LANES), F32),
        vmem((NY, 32, LANES), F32),
        dma((2,)),
        dma((NX, NK)),
        dma((NY, NK)),
        dma((2, 2, R)),
        dma((2, 2, R)),
        dma((2, 2, NZ)),
        dma((2, 2, NY)),
        dma((2, 2, NZ)),
        dma((2, NY)),
        dma((2, NY)),
        dma((2,)),
        dma((2, NY)),
        dma((2, NX)),
        dma((2, 2, R)),
        dma((2, 2, R)),
        dma((2,)),
        dma((2, NZ)),
        dma((2, NY)),
    ]
    output, grad_streams, grad_short, grad_skip, grad_weight = pl.pallas_call(
        functools.partial(kernel, dims),
        out_shape=(
            jax.ShapeDtypeStruct((ROWS, OT), BF16),
            jax.ShapeDtypeStruct(streams.shape, BF16),
            jax.ShapeDtypeStruct(short_filter.shape, F32),
            jax.ShapeDtypeStruct((1, C), F32),
            jax.ShapeDtypeStruct((ROWS, C), F32),
        ),
        in_specs=[whole] * 7,
        out_specs=(whole,) * 5,
        scratch_shapes=scratch,
        compiler_params=pltpu.CompilerParams(
            collective_id=0, has_side_effects=True, vmem_limit_bytes=56 * 1024 * 1024
        ),
        name="mixer",
    )(streams, short_filter, residues, rates, skip.reshape(1, C), out_weight, out_cotangent)
    return output, grad_streams, grad_short, grad_skip.reshape(C), grad_weight


def build(mesh, dims):
    return jax.shard_map(
        functools.partial(shards, dims),
        mesh=mesh,
        in_specs=(
            P(None, "ctx", "tp"),
            P(None, None, "tp"),
            P(None, "tp"),
            P(None, "tp"),
            P("tp"),
            P("ctx", "tp"),
            P("ctx", "tp"),
        ),
        out_specs=(
            P("ctx", "tp"),
            P(None, "ctx", "tp"),
            P(None, None, "tp"),
            P("tp"),
            P("ctx", "tp"),
        ),
        check_vma=False,
    )


def solution(mesh):
    return build(mesh, (4, 4, 8, 2))
```

```python
import functools

import jax
import jax.numpy as jnp
from jax import lax
from jax.experimental import pallas as pl
from jax.experimental.pallas import tpu as pltpu
from jax.sharding import PartitionSpec as P

F32 = jnp.float32
BF16 = jnp.bfloat16
HIGHEST = lax.Precision.HIGHEST
MESH = pl.DeviceIdType.MESH
ROWS = 128
HALF = 64
LANES = 128
MEMBERS = 16
MODES = 16
TAPS = 7
PER_TILE = LANES // MEMBERS


def iota(shape, dim):
    return lax.broadcasted_iota(jnp.int32, shape, dim)


def two_terms(value):
    high = value.astype(BF16)
    return high, (value - high.astype(F32)).astype(BF16)


def kernel(
    dims,
    s_ref,
    sf_ref,
    res_ref,
    rate_ref,
    skip_ref,
    w_ref,
    cot_ref,
    out_ref,
    gs_ref,
    gshort_ref,
    gskip_ref,
    gw_ref,
    xpad,
    rim_in,
    sm,
    mixed,
    field,
    gfb,
    gm,
    tf,
    tb,
    inf,
    inb,
    entf,
    entb,
    rate_ch,
    dec,
    vecs,
    taps,
    prof,
    st_out,
    stz,
    tot,
    ret_out,
    bef,
    wg,
    cotg,
    gg,
    upp,
    up_in,
    outp,
    pair_in,
    outh,
    out_y,
    out_x,
    gwp,
    gw_r,
    gw_l,
    gsp,
    tapsum,
    sml,
    smz,
    smy,
    rim_sem,
    cot_s,
    cot_r,
    cotp_sem,
    wr_sem,
    wl_sem,
    stz_sem,
    tot_sem,
    bef_sem,
    g_sem,
    up_sem,
    pair_sem,
    outy_sem,
    outx_sem,
    gwr_sem,
    gwl_sem,
    grim_sem,
    smz_sem,
    smy_sem,
):
    NX, NY, NZ, NK = dims
    C = s_ref.shape[2]
    G = sf_ref.shape[2]
    OT = cot_ref.shape[1]
    OY = NZ * ROWS
    R = NZ // 2
    HC = C // 2
    c = lax.axis_index("ctx")
    p = lax.axis_index("tp")
    y, z = lax.div(c, NZ), lax.rem(c, NZ)
    x, k = lax.div(p, NK), lax.rem(p, NK)
    last = NY * NZ - 1

    def dev(yy, zz, xx=x, kk=k):
        return (yy * NZ + zz, xx * NK + kk)

    def plus(a, d, n):
        return lax.rem(a + d + n, n)

    def remote(src, dst, ssem, rsem, to):
        return pltpu.make_async_remote_copy(
            src_ref=src, dst_ref=dst, send_sem=ssem, recv_sem=rsem, device_id=to, device_id_type=MESH
        )

    def rows_of(block):
        return pl.ds(pl.multiple_of(block * ROWS, ROWS), ROWS)

    def lanes_of(tile, width=LANES):
        return pl.ds(pl.multiple_of(tile * width, width), width)

    def unless_self(distance, body):
        if distance == 0:
            pl.when(x != y)(body)
        else:
            body()

    barrier = pltpu.get_barrier_semaphore()

    def greet(to):
        pl.semaphore_signal(barrier, inc=1, device_id=to, device_id_type=MESH)

    for d in range(1, NZ):
        greet(dev(y, plus(z, d, NZ)))
    for d in range(1, NY):
        greet(dev(plus(y, d, NY), z))
    for d in range(1, NX):
        greet(dev(y, z, plus(x, d, NX)))
    for d in range(1, NK):
        greet(dev(y, z, x, plus(k, d, NK)))
    for d in range(NX):
        unless_self(d, lambda: greet(dev(x, z, plus(x, d, NX))))
        unless_self(d, lambda: greet(dev(plus(y, d, NY), z, y)))

    @pl.when(c > 0)
    def _():
        greet((c - 1, p))

    @pl.when(c < last)
    def _():
        greet((c + 1, p))

    spread = (lax.div(iota((G, C), 1), MEMBERS) == iota((G, C), 0)).astype(F32)
    rate_ch[...] = jnp.dot(rate_ref[...], spread, precision=HIGHEST, preferred_element_type=F32)
    res_ch = jnp.dot(res_ref[...], spread, precision=HIGHEST, preferred_element_type=F32)
    for i in range(3):
        taps[i, pl.ds(0, TAPS), :] = jnp.dot(
            sf_ref[i], spread, precision=HIGHEST, preferred_element_type=F32
        )
    own_mode = lax.rem(iota((MODES, C), 1), MODES) == iota((MODES, C), 0)
    dec[...] = jnp.exp(-float(ROWS) * rate_ch[...])
    vecs[pl.ds(0, 1), :] = jnp.sum(jnp.where(own_mode, rate_ch[...], 0.0), axis=0, keepdims=True)
    vecs[pl.ds(1, 1), :] = jnp.sum(jnp.where(own_mode, res_ch, 0.0), axis=0, keepdims=True)

    eye = (iota((G, G), 0) == iota((G, G), 1)).astype(F32)
    turned = (((1,), (1,)), ((), ()))
    rate_t = lax.dot_general(eye, rate_ref[...], turned, precision=HIGHEST, preferred_element_type=F32)
    res_t = lax.dot_general(eye, res_ref[...], turned, precision=HIGHEST, preferred_element_type=F32)
    lag = iota((G, LANES), 1).astype(F32)
    ahead = jnp.zeros((G, LANES), F32)
    behind = jnp.zeros((G, LANES), F32)
    for m in range(MODES):
        ahead = ahead + res_t[:, m : m + 1] * jnp.exp(-rate_t[:, m : m + 1] * lag)
        behind = behind + res_t[:, m : m + 1] * jnp.exp(-rate_t[:, m : m + 1] * (ROWS - 1.0 - lag))
    prof[0] = ahead
    prof[1] = behind

    row_id, lane_id = iota((ROWS, LANES), 0), iota((ROWS, LANES), 1)
    lane_group = lax.div(lane_id, MEMBERS)

    def tables(j, carry):
        ls = lanes_of(j)
        rate = vecs[pl.ds(0, 1), ls]
        amp = vecs[pl.ds(1, 1), ls] * jnp.exp(-rate)
        place = row_id.astype(F32)
        early = jnp.exp(-rate * place)
        late = jnp.exp(-rate * (ROWS - 1.0 - place))
        for table, value in ((inf, late), (inb, early)):
            high, low = two_terms(jnp.transpose(value))
            table[j, pl.ds(0, ROWS), :] = high
            table[j, pl.ds(ROWS, ROWS), :] = low
        for table, value in ((entf, amp * early), (entb, amp * late)):
            high, low = two_terms(value)
            table[j, :, pl.ds(0, LANES)] = high
            table[j, :, pl.ds(LANES, LANES)] = low
            table[j, :, pl.ds(2 * LANES, LANES)] = high
        return carry

    def toeplitz(j, carry):
        for g in range(PER_TILE):
            one = prof[0, pl.ds(j * PER_TILE + g, 1), :]
            skew = pltpu.roll(
                jnp.broadcast_to(one, (ROWS, LANES)), 0, 1, stride=1, stride_axis=0
            )
            tb[j, :, pl.ds(g * LANES, LANES)] = jnp.where(lane_id >= row_id, skew, 0.0).astype(BF16)
            one = prof[1, pl.ds(j * PER_TILE + g, 1), :]
            skew = pltpu.roll(
                jnp.broadcast_to(one, (ROWS, LANES)), 1, 1, stride=1, stride_axis=0
            )
            tf[j, :, pl.ds(g * LANES, LANES)] = jnp.where(lane_id <= row_id, skew, 0.0).astype(BF16)
        return carry

    peers = NZ - 1 + NY - 1 + NX - 1 + NK - 1 + 2 * (NX - 1)
    peers = peers + jnp.where(x != y, 2, 0) + jnp.where(c > 0, 1, 0) + jnp.where(c < last, 1, 0)
    pl.semaphore_wait(barrier, peers)

    rim_copy = remote(
        s_ref.at[:, pl.ds(ROWS - 16, 16), :], rim_in, rim_sem.at[0], rim_sem.at[1], (lax.rem(c + 1, last + 1), p)
    )

    @pl.when(c < last)
    def _():
        rim_copy.start()

    right, left = dev(y, plus(z, 1, NZ)), dev(y, plus(z, -1, NZ))
    wg[rows_of(z), :] = w_ref[...]

    def long_way(direction, half):
        return R if direction == half else R - 1

    def half_rows(block, half):
        return pl.ds(pl.multiple_of(block * ROWS + half * HALF, HALF), HALF)

    def w_copy(direction, half, step):
        sem = wr_sem if direction == 0 else wl_sem
        block = wg.at[half_rows(plus(z, -step if direction == 0 else step, NZ), half), :]
        return remote(block, block, sem.at[0, half, step], sem.at[1, half, step], right if direction == 0 else left)

    def w_arrived(step, lap):
        for direction in range(2):
            half = direction if lap == 0 else 1 - direction
            steps = long_way(direction, half)
            if step <= steps:
                sem = wr_sem if direction == 0 else wl_sem
                block = wg.at[half_rows(plus(z, -step if direction == 0 else step, NZ), half), :]
                remote(block, block, sem.at[0, half, step - 1], sem.at[1, half, step - 1], right).wait_recv()
            if step < steps:
                w_copy(direction, half, step).start()

    for lap in range(2):
        for direction in range(2):
            half = direction if lap == 0 else 1 - direction
            if long_way(direction, half) > 0:
                w_copy(direction, half, 0).start()

    def cot_copy(d):
        return remote(
            cot_ref, cotg.at[rows_of(y), lanes_of(k, OT)], cot_s.at[d], cot_r.at[y], dev(x, z, plus(x, d, NX))
        )

    def cot_pair():
        block = cotg.at[:, lanes_of(k, OT)]
        return remote(block, block, cotp_sem.at[0], cotp_sem.at[1], dev(y, z, x, 1 - k))

    for d in range(NX):
        unless_self(d, lambda: cot_copy(d).start())

    @pl.when(x == y)
    def _():
        cotg[rows_of(y), lanes_of(k, OT)] = cot_ref[...]

    lax.fori_loop(0, NZ, tables, 0)

    for i in range(3):
        xpad[i, pl.ds(8, ROWS), :] = s_ref[i].astype(F32)

    @pl.when(c == 0)
    def _():
        rim_in[...] = jnp.zeros_like(rim_in)

    @pl.when(c > 0)
    def _():
        rim_copy.wait_recv()

    for i in range(3):
        xpad[i, pl.ds(0, 8), :] = rim_in[i].astype(F32)[8:16, :]

    def spread_groups(value):
        return jnp.concatenate(
            [jnp.where(lane_group == g, value, 0.0).astype(BF16) for g in range(PER_TILE)], axis=0
        )

    mode_block = lax.div(row_id, MODES) == lane_group

    def state_of(table, value):
        both = jnp.dot(table, value, preferred_element_type=F32)
        both = jnp.where(mode_block, both[:ROWS] + both[ROWS:], 0.0)
        total = both[:MODES]
        for g in range(1, PER_TILE):
            total = total + both[g * MODES : (g + 1) * MODES]
        return total

    def from_state(table, state):
        tall = jnp.where(mode_block, jnp.concatenate([state] * PER_TILE, axis=0), 0.0)
        high, low = two_terms(tall)
        return jnp.dot(
            table, jnp.concatenate([high, high, low], axis=0), preferred_element_type=F32
        )

    def states_out(way):
        stz[way, z] = st_out[way, z]
        for d in range(1, NZ):
            to = plus(z, d, NZ)
            remote(
                st_out.at[way, to], stz.at[way, z], stz_sem.at[way, 0, d], stz_sem.at[way, 1, d], dev(y, to)
            ).start()

    def states_row(way):
        for d in range(1, NZ):
            src = plus(z, -d, NZ)
            remote(
                st_out.at[way, src], stz.at[way, src], stz_sem.at[way, 0, d], stz_sem.at[way, 1, d], dev(y, src)
            ).wait_recv()
        factor = dec[:, lanes_of(z)]
        state = jnp.zeros((MODES, LANES), F32)
        for i in range(NZ):
            at = i if way == 0 else NZ - 1 - i
            ret_out[way, at] = state
            state = factor * state + stz[way, at]
        tot[way, y] = state
        for d in range(1, NY):
            to = plus(y, d, NY)
            remote(
                tot.at[way, y], tot.at[way, y], tot_sem.at[way, 0, d], tot_sem.at[way, 1, d], dev(to, z)
            ).start()

    def states_back(way):
        for d in range(1, NY):
            src = plus(y, -d, NY)
            remote(
                tot.at[way, src], tot.at[way, src], tot_sem.at[way, 0, d], tot_sem.at[way, 1, d], dev(src, z)
            ).wait_recv()
        factor = dec[:, lanes_of(z)]
        row_factor = jnp.exp(-float(ROWS * NZ) * rate_ch[:, lanes_of(z)])
        state = jnp.zeros((MODES, LANES), F32)
        for i in range(NY):
            at = i if way == 0 else NY - 1 - i
            counts = (at < y) if way == 0 else (at > y)
            state = jnp.where(counts, row_factor * state + tot[way, at], state)
        for i in range(NZ):
            at = i if way == 0 else NZ - 1 - i
            ret_out[way, at] = ret_out[way, at] + state
            state = state * factor
        bef[way, z] = ret_out[way, z]
        for d in range(1, NZ):
            to = plus(z, d, NZ)
            remote(
                ret_out.at[way, to], bef.at[way, z], bef_sem.at[way, 0, d], bef_sem.at[way, 1, d], dev(y, to)
            ).start()

    def states_in(way):
        for d in range(1, NZ):
            src = plus(z, -d, NZ)
            remote(
                ret_out.at[way, src], bef.at[way, src], bef_sem.at[way, 0, d], bef_sem.at[way, 1, d], dev(y, src)
            ).wait_recv()

    def smooth(j, carry):
        ls = lanes_of(j)
        for i in range(3):
            total = taps[i, pl.ds(0, 1), ls] * xpad[i, pl.ds(8, ROWS), ls]
            for n in range(1, TAPS):
                total = total + taps[i, pl.ds(n, 1), ls] * xpad[i, pl.ds(8 - n, ROWS), ls]
            sm[i, :, ls] = total
        value = (sm[1, :, ls] * sm[2, :, ls]).astype(BF16)
        mixed[:, ls] = value
        st_out[0, j] = state_of(inf[j], value)
        return carry

    lax.fori_loop(0, NZ, smooth, 0)
    states_out(0)
    w_arrived(1, 0)
    lax.fori_loop(0, NZ, toeplitz, 0)
    w_arrived(1, 1)

    def local_field(j, carry):
        ls = lanes_of(j)
        value = mixed[:, ls].astype(F32)
        field[:, ls] = skip_ref[:, ls] * value + jnp.dot(
            tf[j], spread_groups(value), preferred_element_type=F32
        )
        return carry

    lax.fori_loop(0, R, local_field, 0)
    w_arrived(2, 0)
    states_row(0)
    lax.fori_loop(R, NZ, local_field, 0)
    w_arrived(2, 1)
    states_back(0)
    w_arrived(3, 0)
    for a in range(NY):

        def cot_wait():
            block = cotg.at[pl.ds(a * ROWS, ROWS), lanes_of(k, OT)]
            remote(block, block, cot_s.at[0], cot_r.at[a], right).wait_recv()

        pl.when(jnp.logical_not((x == y) & (y == a)))(cot_wait)
    if NK == 2:
        cot_pair().start()
    w_arrived(3, 1)

    def gate(j, carry):
        ls = lanes_of(j)
        value = field[:, ls] + from_state(entf[j], bef[0, j])
        field[:, ls] = value
        gg[rows_of(y), ls] = (sm[0, :, ls] * value).astype(BF16)
        return carry

    def g_copy(d, half):
        block = gg.at[rows_of(y), pl.ds(half * HC, HC)]
        return remote(block, block, g_sem.at[0, half, d], g_sem.at[1, half, d], dev(plus(y, d, NY), z))

    def gate_half(half):
        lax.fori_loop(half * (NZ // 2), (half + 1) * (NZ // 2), gate, 0)
        for d in range(1, NY):
            g_copy(d, half).start()

    def g_arrived(half):
        for d in range(1, NY):
            block = gg.at[rows_of(plus(y, -d, NY)), pl.ds(half * HC, HC)]
            remote(block, block, g_sem.at[0, half, d], g_sem.at[1, half, d], right).wait_recv()

    states_in(0)
    gate_half(0)
    for n in range(4, R + 1):
        for lap in range(2):
            w_arrived(n, lap)
    if NK == 2:
        other = cotg.at[:, lanes_of(1 - k, OT)]
        remote(other, other, cotp_sem.at[0], cotp_sem.at[1], right).wait_recv()

    WIDE = 256

    def up_part(j, carry):
        ls = lanes_of(j, WIDE)
        upp[:, ls] = jnp.dot(cotg[...], wg[:, ls], preferred_element_type=F32).astype(BF16)
        return carry

    lax.fori_loop(0, C // WIDE, up_part, 0)

    def up_copy(d):
        to = plus(y, d, NY)
        return remote(upp.at[rows_of(to), :], up_in.at[d], up_sem.at[0, d], up_sem.at[1, d], dev(to, z))

    for d in range(1, NY):
        up_copy(d).start()

    gate_half(1)

    over_rows = (((0,), (0,)), ((), ()))

    def gw_part(half):
        def body(i, carry):
            block = lax.rem(z + R + NZ - i, NZ)
            gwp[block, :, pl.ds(half * HC, HC)] = lax.dot_general(
                cotg[:, lanes_of(block)], gg[:, pl.ds(half * HC, HC)], over_rows, preferred_element_type=F32
            ).astype(BF16)
            return carry

        lax.fori_loop(0, NZ, body, 0)

    def gw_block(direction, half, step):
        far = long_way(direction, half) - step
        return plus(z, far if direction == 0 else -far, NZ)

    def gw_copy(direction, half, step):
        sem, into = (gwr_sem, gw_r) if direction == 0 else (gwl_sem, gw_l)
        return remote(
            gwp.at[gw_block(direction, half, step), :, pl.ds(half * HC, HC)],
            into.at[half, step],
            sem.at[0, half, step],
            sem.at[1, half, step],
            right if direction == 0 else left,
        )

    def gw_arrived(step, half):
        cols = pl.ds(half * HC, HC)
        for direction in range(2):
            steps = long_way(direction, half)
            if step <= steps:
                gw_copy(direction, half, step - 1).wait_recv()
            if step < steps:
                at = gw_block(direction, half, step)
                came = gw_r if direction == 0 else gw_l
                gwp[at, :, cols] = (gwp[at, :, cols].astype(F32) + came[half, step - 1].astype(F32)).astype(BF16)
                gw_copy(direction, half, step).start()

    def gw_start(half):
        g_arrived(half)
        gw_part(half)
        for direction in range(2):
            if long_way(direction, half) > 0:
                gw_copy(direction, half, 0).start()

    def out_part(j, carry):
        ls = lanes_of(j, WIDE)
        outp[:, ls] = lax.dot_general(gg[...], wg[ls, :], turned, preferred_element_type=F32).astype(BF16)
        return carry


    def pair_copy():
        return remote(
            outp.at[:, lanes_of(1 - k, OT)], pair_in, pair_sem.at[0], pair_sem.at[1], dev(y, z, x, 1 - k)
        )

    def outy_copy(d):
        to = plus(y, d, NY)
        return remote(outh.at[rows_of(to), :], out_y.at[y], outy_sem.at[0, d], outy_sem.at[1, d], dev(to, z))

    def outx_copy(d):
        to = plus(x, d, NX)
        return remote(out_y.at[to], out_x.at[x], outx_sem.at[0, d], outx_sem.at[1, d], dev(y, z, to))

    def out_over_y():
        if NK == 2:
            pair_copy().wait_recv()
            outh[...] = (outp[:, lanes_of(k, OT)].astype(F32) + pair_in[...].astype(F32)).astype(BF16)
        else:
            outh[...] = outp[...]
        for d in range(1, NY):
            outy_copy(d).start()
        out_y[y] = outh[rows_of(y), :]

    def out_over_x():
        for d in range(1, NY):
            block = out_y.at[plus(y, -d, NY)]
            remote(block, block, outy_sem.at[0, d], outy_sem.at[1, d], right).wait_recv()
        for d in range(1, NX):
            outx_copy(d).start()
        out_x[x] = out_y[x]

    def out_done():
        for d in range(1, NX):
            block = out_x.at[plus(x, -d, NX)]
            remote(block, block, outx_sem.at[0, d], outx_sem.at[1, d], right).wait_recv()
        value = out_x[0].astype(F32)
        for n in range(1, NX):
            value = value + out_x[n].astype(F32)
        out_ref[...] = value.astype(BF16)

    gw_start(0)
    gw_arrived(1, 0)

    for d in range(1, NY):
        up_copy(d).wait_recv()

    def grad_field(j, carry):
        ls = lanes_of(j)
        up = upp[rows_of(y), ls].astype(F32)
        for d in range(1, NY):
            up = up + up_in[d, :, ls].astype(F32)
        gf = up * sm[0, :, ls]
        gsp[0, pl.ds(0, ROWS), ls] = up * field[:, ls]
        gm[:, ls] = skip_ref[:, ls] * gf
        sml[pl.ds(24 + j, 1), :] = jnp.sum(gf * mixed[:, ls].astype(F32), axis=0, keepdims=True)
        value = gf.astype(BF16)
        gfb[:, ls] = value
        st_out[1, j] = state_of(inb[j], value)
        return carry

    lax.fori_loop(0, NZ, grad_field, 0)
    states_out(1)

    def local_grad(j, carry):
        ls = lanes_of(j)
        gm[:, ls] = gm[:, ls] + jnp.dot(
            tb[j], spread_groups(gfb[:, ls].astype(F32)), preferred_element_type=F32
        )
        return carry

    def tap_grad(i, j):
        ls = lanes_of(j)
        value = gsp[i, pl.ds(0, ROWS), ls]
        for n in range(TAPS):
            tapsum[pl.ds(i * TAPS + n, 1), ls] = jnp.sum(
                value * xpad[i, pl.ds(8 - n, ROWS), ls], axis=0, keepdims=True
            )

    gw_arrived(2, 0)
    lax.fori_loop(0, NZ, local_grad, 0)
    gw_start(1)
    states_row(1)
    lax.fori_loop(0, OY // WIDE, out_part, 0)
    if NK == 2:
        pair_copy().start()
    gw_arrived(3, 0)
    states_back(1)
    gw_arrived(1, 1)
    for n in range(4, R + 1):
        gw_arrived(n, 0)

    def first_taps(j, carry):
        tap_grad(0, j)
        return carry

    lax.fori_loop(0, NZ, first_taps, 0)
    out_over_y()
    states_in(1)

    def grad_mixed(j, carry):
        ls = lanes_of(j)
        value = gm[:, ls] + from_state(entb[j], bef[1, j])
        gsp[1, pl.ds(0, ROWS), ls] = value * sm[2, :, ls]
        gsp[2, pl.ds(0, ROWS), ls] = value * sm[1, :, ls]
        return carry

    lax.fori_loop(0, NZ, grad_mixed, 0)

    grim_copy = remote(
        gsp.at[:, pl.ds(0, 8), :],
        gsp.at[:, pl.ds(ROWS, 8), :],
        grim_sem.at[0],
        grim_sem.at[1],
        (lax.rem(c + last, last + 1), p),
    )

    @pl.when(c > 0)
    def _():
        grim_copy.start()

    def other_taps(j, carry):
        tap_grad(1, j)
        tap_grad(2, j)
        return carry

    gw_arrived(2, 1)
    lax.fori_loop(0, NZ, other_taps, 0)
    tapsum[pl.ds(3 * TAPS, 3), :] = jnp.zeros((3, C), F32)
    gather_groups = (lax.div(iota((C, LANES), 0), MEMBERS) == iota((C, LANES), 1)).astype(F32)
    sml[pl.ds(0, 24), :] = jnp.dot(
        tapsum[...], gather_groups, precision=HIGHEST, preferred_element_type=F32
    )

    def small_z(d):
        return remote(sml, smz.at[d], smz_sem.at[0, d], smz_sem.at[1, d], dev(y, plus(z, d, NZ)))

    def small_y(d):
        return remote(smy.at[0], smy.at[d], smy_sem.at[0, d], smy_sem.at[1, d], dev(plus(y, d, NY), z))

    for d in range(1, NZ):
        small_z(d).start()

    @pl.when(c == last)
    def _():
        gsp[:, pl.ds(ROWS, 8), :] = jnp.zeros((3, 8, C), F32)

    @pl.when(c < last)
    def _():
        grim_copy.wait_recv()

    def streams_grad(j, carry):
        ls = lanes_of(j)
        for i in range(3):
            total = taps[i, pl.ds(0, 1), ls] * gsp[i, pl.ds(0, ROWS), ls]
            for n in range(1, TAPS):
                total = total + taps[i, pl.ds(n, 1), ls] * gsp[i, pl.ds(n, ROWS), ls]
            gs_ref[i, :, ls] = total.astype(BF16)
        return carry

    out_over_x()
    gw_arrived(3, 1)
    lax.fori_loop(0, NZ, streams_grad, 0)

    total = sml[...]
    for d in range(1, NZ):
        small_z(d).wait_recv()
        total = total + smz[d]
    smy[0] = total
    for d in range(1, NY):
        small_y(d).start()

    out_done()
    for n in range(4, R + 1):
        gw_arrived(n, 1)
    for half in range(2):
        cols = pl.ds(half * HC, HC)
        mine = gwp[z, :, cols].astype(F32)
        for direction, came in ((0, gw_r), (1, gw_l)):
            if long_way(direction, half) > 0:
                mine = mine + came[half, long_way(direction, half) - 1].astype(F32)
        gw_ref[:, cols] = mine

    total = smy[0]
    for d in range(1, NY):
        small_y(d).wait_recv()
        total = total + smy[d]
    for i in range(3):
        gshort_ref[i] = total[i * TAPS : (i + 1) * TAPS, :G]
    for j in range(NZ):
        gskip_ref[:, pl.ds(j * LANES, LANES)] = total[24 + j : 25 + j, :]

    @pl.when(c < last)
    def _():
        rim_copy.wait_send()

    @pl.when(c > 0)
    def _():
        grim_copy.wait_send()

    for direction in range(2):
        for half in range(2):
            for step in range(long_way(direction, half)):
                w_copy(direction, half, step).wait_send()
                gw_copy(direction, half, step).wait_send()
    for d in range(NX):
        unless_self(d, lambda: cot_copy(d).wait_send())
    if NK == 2:
        cot_pair().wait_send()
        pair_copy().wait_send()
    for d in range(1, NX):
        outx_copy(d).wait_send()
    for d in range(1, NY):
        outy_copy(d).wait_send()
    for d in range(1, NY):
        g_copy(d, 0).wait_send()
        g_copy(d, 1).wait_send()
        up_copy(d).wait_send()
        small_y(d).wait_send()
        for way in range(2):
            remote(tot.at[way, y], tot.at[way, y], tot_sem.at[way, 0, d], tot_sem.at[way, 1, d], right).wait_send()
    for d in range(1, NZ):
        small_z(d).wait_send()
        for way in range(2):
            for buf, sem in ((st_out, stz_sem), (ret_out, bef_sem)):
                block = buf.at[way, plus(z, d, NZ)]
                remote(block, block, sem.at[way, 0, d], sem.at[way, 1, d], right).wait_send()


def hand_over(*refs):
    copies = [pltpu.make_async_copy(refs[i], refs[5 + i], refs[10].at[i]) for i in range(5)]
    for one in copies:
        one.start()
    for one in copies:
        one.wait()


def shards(dims, streams, short_filter, residues, rates, skip, out_weight, out_cotangent):
    NX, NY, NZ, NK = dims
    C = streams.shape[2]
    G = residues.shape[1]
    OT = out_cotangent.shape[1]
    OY = NZ * ROWS
    R = NZ // 2
    vmem = pltpu.VMEM
    dma = pltpu.SemaphoreType.DMA
    whole = pl.BlockSpec(memory_space=pltpu.VMEM)
    scratch = [
        vmem((3, ROWS + 8, C), F32),
        vmem((3, 16, C), BF16),
        vmem((3, ROWS, C), F32),
        vmem((ROWS, C), BF16),
        vmem((ROWS, C), F32),
        vmem((ROWS, C), BF16),
        vmem((ROWS, C), F32),
        vmem((NZ, ROWS, PER_TILE * LANES), BF16),
        vmem((NZ, ROWS, PER_TILE * LANES), BF16),
        vmem((NZ, 2 * ROWS, LANES), BF16),
        vmem((NZ, 2 * ROWS, LANES), BF16),
        vmem((NZ, ROWS, 3 * LANES), BF16),
        vmem((NZ, ROWS, 3 * LANES), BF16),
        vmem((MODES, C), F32),
        vmem((MODES, C), F32),
        vmem((8, C), F32),
        vmem((3, 8, C), F32),
        vmem((2, G, LANES), F32),
        vmem((2, NZ, MODES, LANES), F32),
        vmem((2, NZ, MODES, LANES), F32),
        vmem((2, NY, MODES, LANES), F32),
        vmem((2, NZ, MODES, LANES), F32),
        vmem((2, NZ, MODES, LANES), F32),
        vmem((OY, C), BF16),
        vmem((NY * ROWS, OY), BF16),
        vmem((NY * ROWS, C), BF16),
        vmem((NY * ROWS, C), BF16),
        vmem((NY, ROWS, C), BF16),
        vmem((NY * ROWS, OY), BF16),
        vmem((NY * ROWS, OT), BF16),
        vmem((NY * ROWS, OT), BF16),
        vmem((NY, ROWS, OT), BF16),
        vmem((NX, ROWS, OT), BF16),
        vmem((NZ, ROWS, C), BF16),
        vmem((2, R, ROWS, C // 2), BF16),
        vmem((2, R, ROWS, C // 2), BF16),
        vmem((3, ROWS + 8, C), F32),
        vmem((24, C), F32),
        vmem((32, LANES), F32),
        vmem((NZ, 32, LANES), F32),
        vmem((NY, 32, LANES), F32),
        dma((2,)),
        dma((NX,)),
        dma((NY,)),
        dma((2,)),
        dma((2, 2, R)),
        dma((2, 2, R)),
        dma((2, 2, NZ)),
        dma((2, 2, NY)),
        dma((2, 2, NZ)),
        dma((2, 2, NY)),
        dma((2, NY)),
        dma((2,)),
        dma((2, NY)),
        dma((2, NX)),
        dma((2, 2, R)),
        dma((2, 2, R)),
        dma((2,)),
        dma((2, NZ)),
        dma((2, NY)),
    ]
    output, grad_streams, grad_short, grad_skip, grad_weight = pl.pallas_call(
        functools.partial(kernel, dims),
        out_shape=(
            jax.ShapeDtypeStruct((ROWS, OT), BF16),
            jax.ShapeDtypeStruct(streams.shape, BF16),
            jax.ShapeDtypeStruct(short_filter.shape, F32),
            jax.ShapeDtypeStruct((1, C), F32),
            jax.ShapeDtypeStruct((ROWS, C), F32),
        ),
        in_specs=[whole] * 7,
        out_specs=(whole,) * 5,
        scratch_shapes=scratch,
        compiler_params=pltpu.CompilerParams(
            collective_id=0, has_side_effects=True, vmem_limit_bytes=56 * 1024 * 1024
        ),
        name="mixer",
    )(streams, short_filter, residues, rates, skip.reshape(1, C), out_weight, out_cotangent)
    results = (output, grad_streams, grad_short, grad_skip, grad_weight)
    output, grad_streams, grad_short, grad_skip, grad_weight = pl.pallas_call(
        hand_over,
        out_shape=tuple(jax.ShapeDtypeStruct(a.shape, a.dtype) for a in results),
        in_specs=[whole] * 5,
        out_specs=(pl.BlockSpec(memory_space=pl.ANY),) * 5,
        scratch_shapes=[dma((5,))],
        name="hand_over",
    )(*results)
    return output, grad_streams, grad_short, grad_skip.reshape(C), grad_weight


def build(mesh, dims):
    return jax.shard_map(
        functools.partial(shards, dims),
        mesh=mesh,
        in_specs=(
            P(None, "ctx", "tp"),
            P(None, None, "tp"),
            P(None, "tp"),
            P(None, "tp"),
            P("tp"),
            P("ctx", "tp"),
            P("ctx", "tp"),
        ),
        out_specs=(
            P("ctx", "tp"),
            P(None, "ctx", "tp"),
            P(None, None, "tp"),
            P("tp"),
            P("ctx", "tp"),
        ),
        check_vma=False,
    )


def solution(mesh):
    return build(mesh, (4, 4, 8, 2))
```

```python
import functools

import jax
import jax.numpy as jnp
from jax import lax
from jax.experimental import pallas as pl
from jax.experimental.pallas import tpu as pltpu
from jax.sharding import PartitionSpec as P

F32 = jnp.float32
BF16 = jnp.bfloat16
HIGHEST = lax.Precision.HIGHEST
MESH = pl.DeviceIdType.MESH
ROWS = 128
HALF = 64
LANES = 128
MEMBERS = 16
MODES = 16
TAPS = 7
PER_TILE = LANES // MEMBERS


def iota(shape, dim):
    return lax.broadcasted_iota(jnp.int32, shape, dim)


def two_terms(value):
    high = value.astype(BF16)
    return high, (value - high.astype(F32)).astype(BF16)


def kernel(
    dims,
    s_ref,
    sf_ref,
    res_ref,
    rate_ref,
    skip_ref,
    w_ref,
    cot_ref,
    out_ref,
    gs_ref,
    gshort_ref,
    gskip_ref,
    gw_ref,
    xpad,
    rim_in,
    sm,
    mixed,
    field,
    gfb,
    gm,
    tf,
    tb,
    inf,
    inb,
    entf,
    entb,
    rate_ch,
    dec,
    vecs,
    taps,
    prof,
    st_out,
    stz,
    tot,
    ret_out,
    bef,
    wg,
    cotg,
    gg,
    upp,
    up_in,
    outp,
    pair_in,
    outh,
    out_y,
    out_x,
    gwp,
    gw_r,
    gw_l,
    gsp,
    tapsum,
    sml,
    smz,
    smy,
    rim_sem,
    cot_s,
    cot_r,
    cotp_sem,
    wr_sem,
    wl_sem,
    stz_sem,
    tot_sem,
    bef_sem,
    g_sem,
    up_sem,
    pair_sem,
    outy_sem,
    outx_sem,
    gwr_sem,
    gwl_sem,
    grim_sem,
    smz_sem,
    smy_sem,
):
    NX, NY, NZ, NK = dims
    C = s_ref.shape[2]
    G = sf_ref.shape[2]
    OT = cot_ref.shape[1]
    OY = NZ * ROWS
    R = NZ // 2
    HC = C // 2
    c = lax.axis_index("ctx")
    p = lax.axis_index("tp")
    y, z = lax.div(c, NZ), lax.rem(c, NZ)
    x, k = lax.div(p, NK), lax.rem(p, NK)
    last = NY * NZ - 1

    def dev(yy, zz, xx=x, kk=k):
        return (yy * NZ + zz, xx * NK + kk)

    def plus(a, d, n):
        return lax.rem(a + d + n, n)

    def remote(src, dst, ssem, rsem, to):
        return pltpu.make_async_remote_copy(
            src_ref=src, dst_ref=dst, send_sem=ssem, recv_sem=rsem, device_id=to, device_id_type=MESH
        )

    def rows_of(block):
        return pl.ds(pl.multiple_of(block * ROWS, ROWS), ROWS)

    def lanes_of(tile, width=LANES):
        return pl.ds(pl.multiple_of(tile * width, width), width)

    def unless_self(distance, body):
        if distance == 0:
            pl.when(x != y)(body)
        else:
            body()

    barrier = pltpu.get_barrier_semaphore()

    def greet(to):
        pl.semaphore_signal(barrier, inc=1, device_id=to, device_id_type=MESH)

    for d in range(1, NZ):
        greet(dev(y, plus(z, d, NZ)))
    for d in range(1, NY):
        greet(dev(plus(y, d, NY), z))
    for d in range(1, NX):
        greet(dev(y, z, plus(x, d, NX)))
    for d in range(1, NK):
        greet(dev(y, z, x, plus(k, d, NK)))
    for d in range(NX):
        unless_self(d, lambda: greet(dev(x, z, plus(x, d, NX))))
        unless_self(d, lambda: greet(dev(plus(y, d, NY), z, y)))

    @pl.when(c > 0)
    def _():
        greet((c - 1, p))

    @pl.when(c < last)
    def _():
        greet((c + 1, p))

    spread = (lax.div(iota((G, C), 1), MEMBERS) == iota((G, C), 0)).astype(F32)
    rate_ch[...] = jnp.dot(rate_ref[...], spread, precision=HIGHEST, preferred_element_type=F32)
    res_ch = jnp.dot(res_ref[...], spread, precision=HIGHEST, preferred_element_type=F32)
    for i in range(3):
        taps[i, pl.ds(0, TAPS), :] = jnp.dot(
            sf_ref[i], spread, precision=HIGHEST, preferred_element_type=F32
        )
    own_mode = lax.rem(iota((MODES, C), 1), MODES) == iota((MODES, C), 0)
    dec[...] = jnp.exp(-float(ROWS) * rate_ch[...])
    vecs[pl.ds(0, 1), :] = jnp.sum(jnp.where(own_mode, rate_ch[...], 0.0), axis=0, keepdims=True)
    vecs[pl.ds(1, 1), :] = jnp.sum(jnp.where(own_mode, res_ch, 0.0), axis=0, keepdims=True)

    eye = (iota((G, G), 0) == iota((G, G), 1)).astype(F32)
    turned = (((1,), (1,)), ((), ()))
    rate_t = lax.dot_general(eye, rate_ref[...], turned, precision=HIGHEST, preferred_element_type=F32)
    res_t = lax.dot_general(eye, res_ref[...], turned, precision=HIGHEST, preferred_element_type=F32)
    lag = iota((G, LANES), 1).astype(F32)
    ahead = jnp.zeros((G, LANES), F32)
    behind = jnp.zeros((G, LANES), F32)
    for m in range(MODES):
        ahead = ahead + res_t[:, m : m + 1] * jnp.exp(-rate_t[:, m : m + 1] * lag)
        behind = behind + res_t[:, m : m + 1] * jnp.exp(-rate_t[:, m : m + 1] * (ROWS - 1.0 - lag))
    prof[0] = ahead
    prof[1] = behind

    row_id, lane_id = iota((ROWS, LANES), 0), iota((ROWS, LANES), 1)
    lane_group = lax.div(lane_id, MEMBERS)

    def tables(j, carry):
        ls = lanes_of(j)
        rate = vecs[pl.ds(0, 1), ls]
        amp = vecs[pl.ds(1, 1), ls] * jnp.exp(-rate)
        place = row_id.astype(F32)
        early = jnp.exp(-rate * place)
        late = jnp.exp(-rate * (ROWS - 1.0 - place))
        for table, value in ((inf, late), (inb, early)):
            high, low = two_terms(jnp.transpose(value))
            table[j, pl.ds(0, ROWS), :] = high
            table[j, pl.ds(ROWS, ROWS), :] = low
        for table, value in ((entf, amp * early), (entb, amp * late)):
            high, low = two_terms(value)
            table[j, :, pl.ds(0, LANES)] = high
            table[j, :, pl.ds(LANES, LANES)] = low
            table[j, :, pl.ds(2 * LANES, LANES)] = high
        return carry

    def toeplitz(j, carry):
        for g in range(PER_TILE):
            one = prof[0, pl.ds(j * PER_TILE + g, 1), :]
            skew = pltpu.roll(
                jnp.broadcast_to(one, (ROWS, LANES)), 0, 1, stride=1, stride_axis=0
            )
            tb[j, :, pl.ds(g * LANES, LANES)] = jnp.where(lane_id >= row_id, skew, 0.0).astype(BF16)
            one = prof[1, pl.ds(j * PER_TILE + g, 1), :]
            skew = pltpu.roll(
                jnp.broadcast_to(one, (ROWS, LANES)), 1, 1, stride=1, stride_axis=0
            )
            tf[j, :, pl.ds(g * LANES, LANES)] = jnp.where(lane_id <= row_id, skew, 0.0).astype(BF16)
        return carry

    peers = NZ - 1 + NY - 1 + NX - 1 + NK - 1 + 2 * (NX - 1)
    peers = peers + jnp.where(x != y, 2, 0) + jnp.where(c > 0, 1, 0) + jnp.where(c < last, 1, 0)
    pl.semaphore_wait(barrier, peers)

    rim_copy = remote(
        s_ref.at[:, pl.ds(ROWS - 16, 16), :], rim_in, rim_sem.at[0], rim_sem.at[1], (lax.rem(c + 1, last + 1), p)
    )

    @pl.when(c < last)
    def _():
        rim_copy.start()

    right, left = dev(y, plus(z, 1, NZ)), dev(y, plus(z, -1, NZ))
    wg[rows_of(z), :] = w_ref[...]

    def long_way(direction, half):
        return R if direction == half else R - 1

    def half_rows(block, half):
        return pl.ds(pl.multiple_of(block * ROWS + half * HALF, HALF), HALF)

    def w_copy(direction, half, step):
        sem = wr_sem if direction == 0 else wl_sem
        block = wg.at[half_rows(plus(z, -step if direction == 0 else step, NZ), half), :]
        return remote(block, block, sem.at[0, half, step], sem.at[1, half, step], right if direction == 0 else left)

    def w_arrived(step, lap):
        for direction in range(2):
            half = direction if lap == 0 else 1 - direction
            steps = long_way(direction, half)
            if step <= steps:
                sem = wr_sem if direction == 0 else wl_sem
                block = wg.at[half_rows(plus(z, -step if direction == 0 else step, NZ), half), :]
                remote(block, block, sem.at[0, half, step - 1], sem.at[1, half, step - 1], right).wait_recv()
            if step < steps:
                w_copy(direction, half, step).start()

    for lap in range(2):
        for direction in range(2):
            half = direction if lap == 0 else 1 - direction
            if long_way(direction, half) > 0:
                w_copy(direction, half, 0).start()

    def cot_copy(d):
        return remote(
            cot_ref, cotg.at[rows_of(y), lanes_of(k, OT)], cot_s.at[d], cot_r.at[y], dev(x, z, plus(x, d, NX))
        )

    def cot_pair():
        block = cotg.at[:, lanes_of(k, OT)]
        return remote(block, block, cotp_sem.at[0], cotp_sem.at[1], dev(y, z, x, 1 - k))

    for d in range(NX):
        unless_self(d, lambda: cot_copy(d).start())

    @pl.when(x == y)
    def _():
        cotg[rows_of(y), lanes_of(k, OT)] = cot_ref[...]

    lax.fori_loop(0, NZ, tables, 0)

    for i in range(3):
        xpad[i, pl.ds(8, ROWS), :] = s_ref[i].astype(F32)

    @pl.when(c == 0)
    def _():
        rim_in[...] = jnp.zeros_like(rim_in)

    @pl.when(c > 0)
    def _():
        rim_copy.wait_recv()

    for i in range(3):
        xpad[i, pl.ds(0, 8), :] = rim_in[i].astype(F32)[8:16, :]

    def spread_groups(value):
        return jnp.concatenate(
            [jnp.where(lane_group == g, value, 0.0).astype(BF16) for g in range(PER_TILE)], axis=0
        )

    mode_block = lax.div(row_id, MODES) == lane_group

    def state_of(table, value):
        both = jnp.dot(table, value, preferred_element_type=F32)
        both = jnp.where(mode_block, both[:ROWS] + both[ROWS:], 0.0)
        total = both[:MODES]
        for g in range(1, PER_TILE):
            total = total + both[g * MODES : (g + 1) * MODES]
        return total

    def from_state(table, state):
        tall = jnp.where(mode_block, jnp.concatenate([state] * PER_TILE, axis=0), 0.0)
        high, low = two_terms(tall)
        return jnp.dot(
            table, jnp.concatenate([high, high, low], axis=0), preferred_element_type=F32
        )

    def states_out(way):
        stz[way, z] = st_out[way, z]
        for d in range(1, NZ):
            to = plus(z, d, NZ)
            remote(
                st_out.at[way, to], stz.at[way, z], stz_sem.at[way, 0, d], stz_sem.at[way, 1, d], dev(y, to)
            ).start()

    def states_row(way):
        for d in range(1, NZ):
            src = plus(z, -d, NZ)
            remote(
                st_out.at[way, src], stz.at[way, src], stz_sem.at[way, 0, d], stz_sem.at[way, 1, d], dev(y, src)
            ).wait_recv()
        factor = dec[:, lanes_of(z)]
        state = jnp.zeros((MODES, LANES), F32)
        for i in range(NZ):
            at = i if way == 0 else NZ - 1 - i
            ret_out[way, at] = state
            state = factor * state + stz[way, at]
        tot[way, y] = state
        for d in range(1, NY):
            to = plus(y, d, NY)
            remote(
                tot.at[way, y], tot.at[way, y], tot_sem.at[way, 0, d], tot_sem.at[way, 1, d], dev(to, z)
            ).start()

    def states_back(way):
        for d in range(1, NY):
            src = plus(y, -d, NY)
            remote(
                tot.at[way, src], tot.at[way, src], tot_sem.at[way, 0, d], tot_sem.at[way, 1, d], dev(src, z)
            ).wait_recv()
        factor = dec[:, lanes_of(z)]
        row_factor = jnp.exp(-float(ROWS * NZ) * rate_ch[:, lanes_of(z)])
        state = jnp.zeros((MODES, LANES), F32)
        for i in range(NY):
            at = i if way == 0 else NY - 1 - i
            counts = (at < y) if way == 0 else (at > y)
            state = jnp.where(counts, row_factor * state + tot[way, at], state)
        for i in range(NZ):
            at = i if way == 0 else NZ - 1 - i
            ret_out[way, at] = ret_out[way, at] + state
            state = state * factor
        bef[way, z] = ret_out[way, z]
        for d in range(1, NZ):
            to = plus(z, d, NZ)
            remote(
                ret_out.at[way, to], bef.at[way, z], bef_sem.at[way, 0, d], bef_sem.at[way, 1, d], dev(y, to)
            ).start()

    def states_in(way):
        for d in range(1, NZ):
            src = plus(z, -d, NZ)
            remote(
                ret_out.at[way, src], bef.at[way, src], bef_sem.at[way, 0, d], bef_sem.at[way, 1, d], dev(y, src)
            ).wait_recv()

    def smooth(j, carry):
        ls = lanes_of(j)
        for i in range(3):
            total = taps[i, pl.ds(0, 1), ls] * xpad[i, pl.ds(8, ROWS), ls]
            for n in range(1, TAPS):
                total = total + taps[i, pl.ds(n, 1), ls] * xpad[i, pl.ds(8 - n, ROWS), ls]
            sm[i, :, ls] = total
        value = (sm[1, :, ls] * sm[2, :, ls]).astype(BF16)
        mixed[:, ls] = value
        st_out[0, j] = state_of(inf[j], value)
        return carry

    lax.fori_loop(0, NZ, smooth, 0)
    states_out(0)
    w_arrived(1, 0)
    lax.fori_loop(0, NZ, toeplitz, 0)
    w_arrived(1, 1)

    def local_field(j, carry):
        ls = lanes_of(j)
        value = mixed[:, ls].astype(F32)
        field[:, ls] = skip_ref[:, ls] * value + jnp.dot(
            tf[j], spread_groups(value), preferred_element_type=F32
        )
        return carry

    lax.fori_loop(0, R, local_field, 0)
    states_row(0)
    w_arrived(2, 0)
    lax.fori_loop(R, NZ, local_field, 0)
    states_back(0)
    w_arrived(2, 1)
    w_arrived(3, 0)
    for a in range(NY):

        def cot_wait():
            block = cotg.at[pl.ds(a * ROWS, ROWS), lanes_of(k, OT)]
            remote(block, block, cot_s.at[0], cot_r.at[a], right).wait_recv()

        pl.when(jnp.logical_not((x == y) & (y == a)))(cot_wait)
    if NK == 2:
        cot_pair().start()
    w_arrived(3, 1)

    def gate(j, carry):
        ls = lanes_of(j)
        value = field[:, ls] + from_state(entf[j], bef[0, j])
        field[:, ls] = value
        gg[rows_of(y), ls] = (sm[0, :, ls] * value).astype(BF16)
        return carry

    def g_copy(d, half):
        block = gg.at[rows_of(y), pl.ds(half * HC, HC)]
        return remote(block, block, g_sem.at[0, half, d], g_sem.at[1, half, d], dev(plus(y, d, NY), z))

    def gate_half(half):
        lax.fori_loop(half * (NZ // 2), (half + 1) * (NZ // 2), gate, 0)
        for d in range(1, NY):
            g_copy(d, half).start()

    def g_arrived(half):
        for d in range(1, NY):
            block = gg.at[rows_of(plus(y, -d, NY)), pl.ds(half * HC, HC)]
            remote(block, block, g_sem.at[0, half, d], g_sem.at[1, half, d], right).wait_recv()

    states_in(0)
    gate_half(0)
    for n in range(4, R + 1):
        for lap in range(2):
            w_arrived(n, lap)
    if NK == 2:
        other = cotg.at[:, lanes_of(1 - k, OT)]
        remote(other, other, cotp_sem.at[0], cotp_sem.at[1], right).wait_recv()

    WIDE = 256

    def up_part(j, carry):
        ls = lanes_of(j, WIDE)
        upp[:, ls] = jnp.dot(cotg[...], wg[:, ls], preferred_element_type=F32).astype(BF16)
        return carry

    lax.fori_loop(0, C // WIDE, up_part, 0)

    def up_copy(d):
        to = plus(y, d, NY)
        return remote(upp.at[rows_of(to), :], up_in.at[d], up_sem.at[0, d], up_sem.at[1, d], dev(to, z))

    for d in range(1, NY):
        up_copy(d).start()

    gate_half(1)

    over_rows = (((0,), (0,)), ((), ()))

    def gw_part(half):
        def body(i, carry):
            block = lax.rem(z + R + NZ - i, NZ)
            gwp[block, :, pl.ds(half * HC, HC)] = lax.dot_general(
                cotg[:, lanes_of(block)], gg[:, pl.ds(half * HC, HC)], over_rows, preferred_element_type=F32
            ).astype(BF16)
            return carry

        lax.fori_loop(0, NZ, body, 0)

    def gw_block(direction, half, step):
        far = long_way(direction, half) - step
        return plus(z, far if direction == 0 else -far, NZ)

    def gw_copy(direction, half, step, part):
        sem, into = (gwr_sem, gw_r) if direction == 0 else (gwl_sem, gw_l)
        rows = pl.ds(part * HALF, HALF)
        return remote(
            gwp.at[gw_block(direction, half, step), rows, pl.ds(half * HC, HC)],
            into.at[half, step, rows, :],
            sem.at[0, half, step, part],
            sem.at[1, half, step, part],
            right if direction == 0 else left,
        )

    def gw_arrived(step, half):
        cols = pl.ds(half * HC, HC)
        for part in range(2):
            rows = pl.ds(part * HALF, HALF)
            for direction in range(2):
                steps = long_way(direction, half)
                if step <= steps:
                    gw_copy(direction, half, step - 1, part).wait_recv()
                if step < steps:
                    at = gw_block(direction, half, step)
                    came = gw_r if direction == 0 else gw_l
                    mine = gwp[at, rows, cols].astype(F32)
                    gwp[at, rows, cols] = (mine + came[half, step - 1, rows, :].astype(F32)).astype(BF16)
                    gw_copy(direction, half, step, part).start()

    def gw_start(half):
        g_arrived(half)
        gw_part(half)
        for direction in range(2):
            if long_way(direction, half) > 0:
                for part in range(2):
                    gw_copy(direction, half, 0, part).start()

    def out_part(j, carry):
        ls = lanes_of(j, WIDE)
        outp[:, ls] = lax.dot_general(gg[...], wg[ls, :], turned, preferred_element_type=F32).astype(BF16)
        return carry


    def pair_copy():
        return remote(
            outp.at[:, lanes_of(1 - k, OT)], pair_in, pair_sem.at[0], pair_sem.at[1], dev(y, z, x, 1 - k)
        )

    def outy_copy(d):
        to = plus(y, d, NY)
        return remote(outh.at[rows_of(to), :], out_y.at[y], outy_sem.at[0, d], outy_sem.at[1, d], dev(to, z))

    def outx_copy(d):
        to = plus(x, d, NX)
        return remote(out_y.at[to], out_x.at[x], outx_sem.at[0, d], outx_sem.at[1, d], dev(y, z, to))

    def out_over_y():
        if NK == 2:
            pair_copy().wait_recv()
            outh[...] = (outp[:, lanes_of(k, OT)].astype(F32) + pair_in[...].astype(F32)).astype(BF16)
        else:
            outh[...] = outp[...]
        for d in range(1, NY):
            outy_copy(d).start()
        out_y[y] = outh[rows_of(y), :]

    def out_over_x():
        for d in range(1, NY):
            block = out_y.at[plus(y, -d, NY)]
            remote(block, block, outy_sem.at[0, d], outy_sem.at[1, d], right).wait_recv()
        for d in range(1, NX):
            outx_copy(d).start()
        out_x[x] = out_y[x]

    def out_done():
        for d in range(1, NX):
            block = out_x.at[plus(x, -d, NX)]
            remote(block, block, outx_sem.at[0, d], outx_sem.at[1, d], right).wait_recv()
        value = out_x[0].astype(F32)
        for n in range(1, NX):
            value = value + out_x[n].astype(F32)
        out_ref[...] = value.astype(BF16)

    gw_start(0)
    gw_arrived(1, 0)

    for d in range(1, NY):
        up_copy(d).wait_recv()

    def grad_field(j, carry):
        ls = lanes_of(j)
        up = upp[rows_of(y), ls].astype(F32)
        for d in range(1, NY):
            up = up + up_in[d, :, ls].astype(F32)
        gf = up * sm[0, :, ls]
        gsp[0, pl.ds(0, ROWS), ls] = up * field[:, ls]
        gm[:, ls] = skip_ref[:, ls] * gf
        sml[pl.ds(24 + j, 1), :] = jnp.sum(gf * mixed[:, ls].astype(F32), axis=0, keepdims=True)
        value = gf.astype(BF16)
        gfb[:, ls] = value
        st_out[1, j] = state_of(inb[j], value)
        return carry

    lax.fori_loop(0, NZ, grad_field, 0)
    states_out(1)

    def local_grad(j, carry):
        ls = lanes_of(j)
        gm[:, ls] = gm[:, ls] + jnp.dot(
            tb[j], spread_groups(gfb[:, ls].astype(F32)), preferred_element_type=F32
        )
        return carry

    def tap_grad(i, j):
        ls = lanes_of(j)
        value = gsp[i, pl.ds(0, ROWS), ls]
        for n in range(TAPS):
            tapsum[pl.ds(i * TAPS + n, 1), ls] = jnp.sum(
                value * xpad[i, pl.ds(8 - n, ROWS), ls], axis=0, keepdims=True
            )

    gw_arrived(2, 0)
    lax.fori_loop(0, NZ, local_grad, 0)
    gw_start(1)
    states_row(1)
    lax.fori_loop(0, OY // WIDE, out_part, 0)
    if NK == 2:
        pair_copy().start()
    gw_arrived(3, 0)
    states_back(1)
    gw_arrived(1, 1)
    for n in range(4, R + 1):
        gw_arrived(n, 0)

    def first_taps(j, carry):
        tap_grad(0, j)
        return carry

    lax.fori_loop(0, NZ, first_taps, 0)
    out_over_y()
    states_in(1)

    def grad_mixed(j, carry):
        ls = lanes_of(j)
        value = gm[:, ls] + from_state(entb[j], bef[1, j])
        gsp[1, pl.ds(0, ROWS), ls] = value * sm[2, :, ls]
        gsp[2, pl.ds(0, ROWS), ls] = value * sm[1, :, ls]
        return carry

    lax.fori_loop(0, NZ, grad_mixed, 0)

    grim_copy = remote(
        gsp.at[:, pl.ds(0, 8), :],
        gsp.at[:, pl.ds(ROWS, 8), :],
        grim_sem.at[0],
        grim_sem.at[1],
        (lax.rem(c + last, last + 1), p),
    )

    @pl.when(c > 0)
    def _():
        grim_copy.start()

    def other_taps(j, carry):
        tap_grad(1, j)
        tap_grad(2, j)
        return carry

    gw_arrived(2, 1)
    lax.fori_loop(0, NZ, other_taps, 0)
    tapsum[pl.ds(3 * TAPS, 3), :] = jnp.zeros((3, C), F32)
    gather_groups = (lax.div(iota((C, LANES), 0), MEMBERS) == iota((C, LANES), 1)).astype(F32)
    sml[pl.ds(0, 24), :] = jnp.dot(
        tapsum[...], gather_groups, precision=HIGHEST, preferred_element_type=F32
    )

    def small_z(d):
        return remote(sml, smz.at[d], smz_sem.at[0, d], smz_sem.at[1, d], dev(y, plus(z, d, NZ)))

    def small_y(d):
        return remote(smy.at[0], smy.at[d], smy_sem.at[0, d], smy_sem.at[1, d], dev(plus(y, d, NY), z))

    for d in range(1, NZ):
        small_z(d).start()

    @pl.when(c == last)
    def _():
        gsp[:, pl.ds(ROWS, 8), :] = jnp.zeros((3, 8, C), F32)

    @pl.when(c < last)
    def _():
        grim_copy.wait_recv()

    def streams_grad(j, carry):
        ls = lanes_of(j)
        for i in range(3):
            total = taps[i, pl.ds(0, 1), ls] * gsp[i, pl.ds(0, ROWS), ls]
            for n in range(1, TAPS):
                total = total + taps[i, pl.ds(n, 1), ls] * gsp[i, pl.ds(n, ROWS), ls]
            gs_ref[i, :, ls] = total.astype(BF16)
        return carry

    out_over_x()
    gw_arrived(3, 1)
    lax.fori_loop(0, NZ, streams_grad, 0)

    total = sml[...]
    for d in range(1, NZ):
        small_z(d).wait_recv()
        total = total + smz[d]
    smy[0] = total
    for d in range(1, NY):
        small_y(d).start()

    out_done()
    for n in range(4, R + 1):
        gw_arrived(n, 1)
    for half in range(2):
        cols = pl.ds(half * HC, HC)
        mine = gwp[z, :, cols].astype(F32)
        for direction, came in ((0, gw_r), (1, gw_l)):
            if long_way(direction, half) > 0:
                mine = mine + came[half, long_way(direction, half) - 1].astype(F32)
        gw_ref[:, cols] = mine

    total = smy[0]
    for d in range(1, NY):
        small_y(d).wait_recv()
        total = total + smy[d]
    for i in range(3):
        gshort_ref[i] = total[i * TAPS : (i + 1) * TAPS, :G]
    for j in range(NZ):
        gskip_ref[:, pl.ds(j * LANES, LANES)] = total[24 + j : 25 + j, :]

    @pl.when(c < last)
    def _():
        rim_copy.wait_send()

    @pl.when(c > 0)
    def _():
        grim_copy.wait_send()

    for direction in range(2):
        for half in range(2):
            for step in range(long_way(direction, half)):
                w_copy(direction, half, step).wait_send()
                gw_copy(direction, half, step, 0).wait_send()
                gw_copy(direction, half, step, 1).wait_send()
    for d in range(NX):
        unless_self(d, lambda: cot_copy(d).wait_send())
    if NK == 2:
        cot_pair().wait_send()
        pair_copy().wait_send()
    for d in range(1, NX):
        outx_copy(d).wait_send()
    for d in range(1, NY):
        outy_copy(d).wait_send()
    for d in range(1, NY):
        g_copy(d, 0).wait_send()
        g_copy(d, 1).wait_send()
        up_copy(d).wait_send()
        small_y(d).wait_send()
        for way in range(2):
            remote(tot.at[way, y], tot.at[way, y], tot_sem.at[way, 0, d], tot_sem.at[way, 1, d], right).wait_send()
    for d in range(1, NZ):
        small_z(d).wait_send()
        for way in range(2):
            for buf, sem in ((st_out, stz_sem), (ret_out, bef_sem)):
                block = buf.at[way, plus(z, d, NZ)]
                remote(block, block, sem.at[way, 0, d], sem.at[way, 1, d], right).wait_send()


def hand_over(*refs):
    copies = [pltpu.make_async_copy(refs[i], refs[5 + i], refs[10].at[i]) for i in range(5)]
    for one in copies:
        one.start()
    for one in copies:
        one.wait()


def shards(dims, streams, short_filter, residues, rates, skip, out_weight, out_cotangent):
    NX, NY, NZ, NK = dims
    C = streams.shape[2]
    G = residues.shape[1]
    OT = out_cotangent.shape[1]
    OY = NZ * ROWS
    R = NZ // 2
    vmem = pltpu.VMEM
    dma = pltpu.SemaphoreType.DMA
    whole = pl.BlockSpec(memory_space=pltpu.VMEM)
    scratch = [
        vmem((3, ROWS + 8, C), F32),
        vmem((3, 16, C), BF16),
        vmem((3, ROWS, C), F32),
        vmem((ROWS, C), BF16),
        vmem((ROWS, C), F32),
        vmem((ROWS, C), BF16),
        vmem((ROWS, C), F32),
        vmem((NZ, ROWS, PER_TILE * LANES), BF16),
        vmem((NZ, ROWS, PER_TILE * LANES), BF16),
        vmem((NZ, 2 * ROWS, LANES), BF16),
        vmem((NZ, 2 * ROWS, LANES), BF16),
        vmem((NZ, ROWS, 3 * LANES), BF16),
        vmem((NZ, ROWS, 3 * LANES), BF16),
        vmem((MODES, C), F32),
        vmem((MODES, C), F32),
        vmem((8, C), F32),
        vmem((3, 8, C), F32),
        vmem((2, G, LANES), F32),
        vmem((2, NZ, MODES, LANES), F32),
        vmem((2, NZ, MODES, LANES), F32),
        vmem((2, NY, MODES, LANES), F32),
        vmem((2, NZ, MODES, LANES), F32),
        vmem((2, NZ, MODES, LANES), F32),
        vmem((OY, C), BF16),
        vmem((NY * ROWS, OY), BF16),
        vmem((NY * ROWS, C), BF16),
        vmem((NY * ROWS, C), BF16),
        vmem((NY, ROWS, C), BF16),
        vmem((NY * ROWS, OY), BF16),
        vmem((NY * ROWS, OT), BF16),
        vmem((NY * ROWS, OT), BF16),
        vmem((NY, ROWS, OT), BF16),
        vmem((NX, ROWS, OT), BF16),
        vmem((NZ, ROWS, C), BF16),
        vmem((2, R, ROWS, C // 2), BF16),
        vmem((2, R, ROWS, C // 2), BF16),
        vmem((3, ROWS + 8, C), F32),
        vmem((24, C), F32),
        vmem((32, LANES), F32),
        vmem((NZ, 32, LANES), F32),
        vmem((NY, 32, LANES), F32),
        dma((2,)),
        dma((NX,)),
        dma((NY,)),
        dma((2,)),
        dma((2, 2, R)),
        dma((2, 2, R)),
        dma((2, 2, NZ)),
        dma((2, 2, NY)),
        dma((2, 2, NZ)),
        dma((2, 2, NY)),
        dma((2, NY)),
        dma((2,)),
        dma((2, NY)),
        dma((2, NX)),
        dma((2, 2, R, 2)),
        dma((2, 2, R, 2)),
        dma((2,)),
        dma((2, NZ)),
        dma((2, NY)),
    ]
    output, grad_streams, grad_short, grad_skip, grad_weight = pl.pallas_call(
        functools.partial(kernel, dims),
        out_shape=(
            jax.ShapeDtypeStruct((ROWS, OT), BF16),
            jax.ShapeDtypeStruct(streams.shape, BF16),
            jax.ShapeDtypeStruct(short_filter.shape, F32),
            jax.ShapeDtypeStruct((1, C), F32),
            jax.ShapeDtypeStruct((ROWS, C), F32),
        ),
        in_specs=[whole] * 7,
        out_specs=(whole,) * 5,
        scratch_shapes=scratch,
        compiler_params=pltpu.CompilerParams(
            collective_id=0, has_side_effects=True, vmem_limit_bytes=56 * 1024 * 1024
        ),
        name="mixer",
    )(streams, short_filter, residues, rates, skip.reshape(1, C), out_weight, out_cotangent)
    results = (output, grad_streams, grad_short, grad_skip, grad_weight)
    output, grad_streams, grad_short, grad_skip, grad_weight = pl.pallas_call(
        hand_over,
        out_shape=tuple(jax.ShapeDtypeStruct(a.shape, a.dtype) for a in results),
        in_specs=[whole] * 5,
        out_specs=(pl.BlockSpec(memory_space=pl.ANY),) * 5,
        scratch_shapes=[dma((5,))],
        name="hand_over",
    )(*results)
    return output, grad_streams, grad_short, grad_skip.reshape(C), grad_weight


def build(mesh, dims):
    return jax.shard_map(
        functools.partial(shards, dims),
        mesh=mesh,
        in_specs=(
            P(None, "ctx", "tp"),
            P(None, None, "tp"),
            P(None, "tp"),
            P(None, "tp"),
            P("tp"),
            P("ctx", "tp"),
            P("ctx", "tp"),
        ),
        out_specs=(
            P("ctx", "tp"),
            P(None, "ctx", "tp"),
            P(None, None, "tp"),
            P("tp"),
            P("ctx", "tp"),
        ),
        check_vma=False,
    )


def solution(mesh):
    return build(mesh, (4, 4, 8, 2))
```

```python
import functools

import jax
import jax.numpy as jnp
from jax import lax
from jax.experimental import pallas as pl
from jax.experimental.pallas import tpu as pltpu
from jax.sharding import PartitionSpec as P

F32 = jnp.float32
BF16 = jnp.bfloat16
HIGHEST = lax.Precision.HIGHEST
MESH = pl.DeviceIdType.MESH
ROWS = 128
HALF = 64
LANES = 128
MEMBERS = 16
MODES = 16
TAPS = 7
PER_TILE = LANES // MEMBERS


def iota(shape, dim):
    return lax.broadcasted_iota(jnp.int32, shape, dim)


def two_terms(value):
    high = value.astype(BF16)
    return high, (value - high.astype(F32)).astype(BF16)


def kernel(
    dims,
    s_ref,
    sf_ref,
    res_ref,
    rate_ref,
    skip_ref,
    w_ref,
    cot_ref,
    out_ref,
    gs_ref,
    gshort_ref,
    gskip_ref,
    gw_ref,
    xpad,
    rim_in,
    sm,
    mixed,
    field,
    gfb,
    gm,
    tf,
    tb,
    inf,
    inb,
    entf,
    entb,
    rate_ch,
    dec,
    vecs,
    taps,
    prof,
    st_out,
    stz,
    tot,
    ret_out,
    bef,
    wg,
    cotg,
    gg,
    upp,
    up_in,
    outp,
    pair_in,
    outh,
    out_y,
    out_x,
    gwp,
    gw_r,
    gw_l,
    gsp,
    tapsum,
    sml,
    smz,
    smy,
    rim_sem,
    cot_s,
    cot_r,
    cotp_sem,
    wr_sem,
    wl_sem,
    stz_sem,
    tot_sem,
    bef_sem,
    g_sem,
    up_sem,
    pair_sem,
    outy_sem,
    outx_sem,
    gwr_sem,
    gwl_sem,
    grim_sem,
    smz_sem,
    smy_sem,
):
    NX, NY, NZ, NK = dims
    C = s_ref.shape[2]
    G = sf_ref.shape[2]
    OT = cot_ref.shape[1]
    OY = NZ * ROWS
    R = NZ // 2
    HC = C // 2
    c = lax.axis_index("ctx")
    p = lax.axis_index("tp")
    y, z = lax.div(c, NZ), lax.rem(c, NZ)
    x, k = lax.div(p, NK), lax.rem(p, NK)
    last = NY * NZ - 1

    def dev(yy, zz, xx=x, kk=k):
        return (yy * NZ + zz, xx * NK + kk)

    def plus(a, d, n):
        return lax.rem(a + d + n, n)

    def remote(src, dst, ssem, rsem, to):
        return pltpu.make_async_remote_copy(
            src_ref=src, dst_ref=dst, send_sem=ssem, recv_sem=rsem, device_id=to, device_id_type=MESH
        )

    def rows_of(block):
        return pl.ds(pl.multiple_of(block * ROWS, ROWS), ROWS)

    def lanes_of(tile, width=LANES):
        return pl.ds(pl.multiple_of(tile * width, width), width)

    def unless_self(distance, body):
        if distance == 0:
            pl.when(x != y)(body)
        else:
            body()

    barrier = pltpu.get_barrier_semaphore()

    def greet(to):
        pl.semaphore_signal(barrier, inc=1, device_id=to, device_id_type=MESH)

    for d in range(1, NZ):
        greet(dev(y, plus(z, d, NZ)))
    for d in range(1, NY):
        greet(dev(plus(y, d, NY), z))
    for d in range(1, NX):
        greet(dev(y, z, plus(x, d, NX)))
    for d in range(1, NK):
        greet(dev(y, z, x, plus(k, d, NK)))
    for d in range(NX):
        unless_self(d, lambda: greet(dev(x, z, plus(x, d, NX))))
        unless_self(d, lambda: greet(dev(plus(y, d, NY), z, y)))

    @pl.when(c > 0)
    def _():
        greet((c - 1, p))

    @pl.when(c < last)
    def _():
        greet((c + 1, p))

    spread = (lax.div(iota((G, C), 1), MEMBERS) == iota((G, C), 0)).astype(F32)
    rate_ch[...] = jnp.dot(rate_ref[...], spread, precision=HIGHEST, preferred_element_type=F32)
    res_ch = jnp.dot(res_ref[...], spread, precision=HIGHEST, preferred_element_type=F32)
    for i in range(3):
        taps[i, pl.ds(0, TAPS), :] = jnp.dot(
            sf_ref[i], spread, precision=HIGHEST, preferred_element_type=F32
        )
    own_mode = lax.rem(iota((MODES, C), 1), MODES) == iota((MODES, C), 0)
    dec[...] = jnp.exp(-float(ROWS) * rate_ch[...])
    vecs[pl.ds(0, 1), :] = jnp.sum(jnp.where(own_mode, rate_ch[...], 0.0), axis=0, keepdims=True)
    vecs[pl.ds(1, 1), :] = jnp.sum(jnp.where(own_mode, res_ch, 0.0), axis=0, keepdims=True)

    eye = (iota((G, G), 0) == iota((G, G), 1)).astype(F32)
    turned = (((1,), (1,)), ((), ()))
    rate_t = lax.dot_general(eye, rate_ref[...], turned, precision=HIGHEST, preferred_element_type=F32)
    res_t = lax.dot_general(eye, res_ref[...], turned, precision=HIGHEST, preferred_element_type=F32)
    lag = iota((G, LANES), 1).astype(F32)
    ahead = jnp.zeros((G, LANES), F32)
    behind = jnp.zeros((G, LANES), F32)
    for m in range(MODES):
        ahead = ahead + res_t[:, m : m + 1] * jnp.exp(-rate_t[:, m : m + 1] * lag)
        behind = behind + res_t[:, m : m + 1] * jnp.exp(-rate_t[:, m : m + 1] * (ROWS - 1.0 - lag))
    prof[0] = ahead
    prof[1] = behind

    row_id, lane_id = iota((ROWS, LANES), 0), iota((ROWS, LANES), 1)
    lane_group = lax.div(lane_id, MEMBERS)

    def tables(j, carry):
        ls = lanes_of(j)
        rate = vecs[pl.ds(0, 1), ls]
        amp = vecs[pl.ds(1, 1), ls] * jnp.exp(-rate)
        place = row_id.astype(F32)
        early = jnp.exp(-rate * place)
        late = jnp.exp(-rate * (ROWS - 1.0 - place))
        for table, value in ((inf, late), (inb, early)):
            high, low = two_terms(jnp.transpose(value))
            table[j, pl.ds(0, ROWS), :] = high
            table[j, pl.ds(ROWS, ROWS), :] = low
        for table, value in ((entf, amp * early), (entb, amp * late)):
            high, low = two_terms(value)
            table[j, :, pl.ds(0, LANES)] = high
            table[j, :, pl.ds(LANES, LANES)] = low
            table[j, :, pl.ds(2 * LANES, LANES)] = high
        return carry

    def toeplitz(j, carry):
        for g in range(PER_TILE):
            one = prof[0, pl.ds(j * PER_TILE + g, 1), :]
            skew = pltpu.roll(
                jnp.broadcast_to(one, (ROWS, LANES)), 0, 1, stride=1, stride_axis=0
            )
            tb[j, :, pl.ds(g * LANES, LANES)] = jnp.where(lane_id >= row_id, skew, 0.0).astype(BF16)
            one = prof[1, pl.ds(j * PER_TILE + g, 1), :]
            skew = pltpu.roll(
                jnp.broadcast_to(one, (ROWS, LANES)), 1, 1, stride=1, stride_axis=0
            )
            tf[j, :, pl.ds(g * LANES, LANES)] = jnp.where(lane_id <= row_id, skew, 0.0).astype(BF16)
        return carry

    peers = NZ - 1 + NY - 1 + NX - 1 + NK - 1 + 2 * (NX - 1)
    peers = peers + jnp.where(x != y, 2, 0) + jnp.where(c > 0, 1, 0) + jnp.where(c < last, 1, 0)
    pl.semaphore_wait(barrier, peers)

    rim_copy = remote(
        s_ref.at[:, pl.ds(ROWS - 16, 16), :], rim_in, rim_sem.at[0], rim_sem.at[1], (lax.rem(c + 1, last + 1), p)
    )

    @pl.when(c < last)
    def _():
        rim_copy.start()

    right, left = dev(y, plus(z, 1, NZ)), dev(y, plus(z, -1, NZ))
    wg[rows_of(z), :] = w_ref[...]

    def long_way(direction, half):
        return R if direction == half else R - 1

    def half_rows(block, half):
        return pl.ds(pl.multiple_of(block * ROWS + half * HALF, HALF), HALF)

    def w_copy(direction, half, step):
        sem = wr_sem if direction == 0 else wl_sem
        block = wg.at[half_rows(plus(z, -step if direction == 0 else step, NZ), half), :]
        return remote(block, block, sem.at[0, half, step], sem.at[1, half, step], right if direction == 0 else left)

    def w_arrived(step, lap):
        for direction in range(2):
            half = direction if lap == 0 else 1 - direction
            steps = long_way(direction, half)
            if step <= steps:
                sem = wr_sem if direction == 0 else wl_sem
                block = wg.at[half_rows(plus(z, -step if direction == 0 else step, NZ), half), :]
                remote(block, block, sem.at[0, half, step - 1], sem.at[1, half, step - 1], right).wait_recv()
            if step < steps:
                w_copy(direction, half, step).start()

    for lap in range(2):
        for direction in range(2):
            half = direction if lap == 0 else 1 - direction
            if long_way(direction, half) > 0:
                w_copy(direction, half, 0).start()

    def cot_copy(d):
        return remote(
            cot_ref, cotg.at[rows_of(y), lanes_of(k, OT)], cot_s.at[d], cot_r.at[y], dev(x, z, plus(x, d, NX))
        )

    def cot_pair():
        block = cotg.at[:, lanes_of(k, OT)]
        return remote(block, block, cotp_sem.at[0], cotp_sem.at[1], dev(y, z, x, 1 - k))

    for d in range(NX):
        unless_self(d, lambda: cot_copy(d).start())

    @pl.when(x == y)
    def _():
        cotg[rows_of(y), lanes_of(k, OT)] = cot_ref[...]

    lax.fori_loop(0, NZ, tables, 0)

    for i in range(3):
        xpad[i, pl.ds(8, ROWS), :] = s_ref[i].astype(F32)

    @pl.when(c == 0)
    def _():
        rim_in[...] = jnp.zeros_like(rim_in)

    @pl.when(c > 0)
    def _():
        rim_copy.wait_recv()

    for i in range(3):
        xpad[i, pl.ds(0, 8), :] = rim_in[i].astype(F32)[8:16, :]

    def spread_groups(value):
        return jnp.concatenate(
            [jnp.where(lane_group == g, value, 0.0).astype(BF16) for g in range(PER_TILE)], axis=0
        )

    mode_block = lax.div(row_id, MODES) == lane_group

    def state_of(table, value):
        both = jnp.dot(table, value, preferred_element_type=F32)
        both = jnp.where(mode_block, both[:ROWS] + both[ROWS:], 0.0)
        total = both[:MODES]
        for g in range(1, PER_TILE):
            total = total + both[g * MODES : (g + 1) * MODES]
        return total

    def from_state(table, state):
        tall = jnp.where(mode_block, jnp.concatenate([state] * PER_TILE, axis=0), 0.0)
        high, low = two_terms(tall)
        return jnp.dot(
            table, jnp.concatenate([high, high, low], axis=0), preferred_element_type=F32
        )

    def states_out(way):
        stz[way, z] = st_out[way, z]
        for d in range(1, NZ):
            to = plus(z, d, NZ)
            remote(
                st_out.at[way, to], stz.at[way, z], stz_sem.at[way, 0, d], stz_sem.at[way, 1, d], dev(y, to)
            ).start()

    def states_row(way):
        for d in range(1, NZ):
            src = plus(z, -d, NZ)
            remote(
                st_out.at[way, src], stz.at[way, src], stz_sem.at[way, 0, d], stz_sem.at[way, 1, d], dev(y, src)
            ).wait_recv()
        factor = dec[:, lanes_of(z)]
        state = jnp.zeros((MODES, LANES), F32)
        for i in range(NZ):
            at = i if way == 0 else NZ - 1 - i
            ret_out[way, at] = state
            state = factor * state + stz[way, at]
        tot[way, y] = state
        for d in range(1, NY):
            to = plus(y, d, NY)
            remote(
                tot.at[way, y], tot.at[way, y], tot_sem.at[way, 0, d], tot_sem.at[way, 1, d], dev(to, z)
            ).start()

    def states_back(way):
        for d in range(1, NY):
            src = plus(y, -d, NY)
            remote(
                tot.at[way, src], tot.at[way, src], tot_sem.at[way, 0, d], tot_sem.at[way, 1, d], dev(src, z)
            ).wait_recv()
        factor = dec[:, lanes_of(z)]
        row_factor = jnp.exp(-float(ROWS * NZ) * rate_ch[:, lanes_of(z)])
        state = jnp.zeros((MODES, LANES), F32)
        for i in range(NY):
            at = i if way == 0 else NY - 1 - i
            counts = (at < y) if way == 0 else (at > y)
            state = jnp.where(counts, row_factor * state + tot[way, at], state)
        for i in range(NZ):
            at = i if way == 0 else NZ - 1 - i
            ret_out[way, at] = ret_out[way, at] + state
            state = state * factor
        bef[way, z] = ret_out[way, z]
        for d in range(1, NZ):
            to = plus(z, d, NZ)
            remote(
                ret_out.at[way, to], bef.at[way, z], bef_sem.at[way, 0, d], bef_sem.at[way, 1, d], dev(y, to)
            ).start()

    def states_in(way):
        for d in range(1, NZ):
            src = plus(z, -d, NZ)
            remote(
                ret_out.at[way, src], bef.at[way, src], bef_sem.at[way, 0, d], bef_sem.at[way, 1, d], dev(y, src)
            ).wait_recv()

    def smooth(j, carry):
        ls = lanes_of(j)
        for i in range(3):
            total = taps[i, pl.ds(0, 1), ls] * xpad[i, pl.ds(8, ROWS), ls]
            for n in range(1, TAPS):
                total = total + taps[i, pl.ds(n, 1), ls] * xpad[i, pl.ds(8 - n, ROWS), ls]
            sm[i, :, ls] = total
        value = (sm[1, :, ls] * sm[2, :, ls]).astype(BF16)
        mixed[:, ls] = value
        st_out[0, j] = state_of(inf[j], value)
        return carry

    lax.fori_loop(0, NZ, smooth, 0)
    states_out(0)
    w_arrived(1, 0)
    lax.fori_loop(0, NZ, toeplitz, 0)
    w_arrived(1, 1)

    def local_field(j, carry):
        ls = lanes_of(j)
        value = mixed[:, ls].astype(F32)
        field[:, ls] = skip_ref[:, ls] * value + jnp.dot(
            tf[j], spread_groups(value), preferred_element_type=F32
        )
        return carry

    lax.fori_loop(0, R, local_field, 0)
    states_row(0)
    w_arrived(2, 0)
    lax.fori_loop(R, NZ, local_field, 0)
    states_back(0)
    w_arrived(2, 1)
    w_arrived(3, 0)
    for a in range(NY):

        def cot_wait():
            block = cotg.at[pl.ds(a * ROWS, ROWS), lanes_of(k, OT)]
            remote(block, block, cot_s.at[0], cot_r.at[a], right).wait_recv()

        pl.when(jnp.logical_not((x == y) & (y == a)))(cot_wait)
    if NK == 2:
        cot_pair().start()
    w_arrived(3, 1)

    def gate(j, carry):
        ls = lanes_of(j)
        value = field[:, ls] + from_state(entf[j], bef[0, j])
        field[:, ls] = value
        gg[rows_of(y), ls] = (sm[0, :, ls] * value).astype(BF16)
        return carry

    def g_copy(d, half):
        block = gg.at[rows_of(y), pl.ds(half * HC, HC)]
        return remote(block, block, g_sem.at[0, half, d], g_sem.at[1, half, d], dev(plus(y, d, NY), z))

    def gate_half(half):
        lax.fori_loop(half * (NZ // 2), (half + 1) * (NZ // 2), gate, 0)
        for d in range(1, NY):
            g_copy(d, half).start()

    def g_arrived(half):
        for d in range(1, NY):
            block = gg.at[rows_of(plus(y, -d, NY)), pl.ds(half * HC, HC)]
            remote(block, block, g_sem.at[0, half, d], g_sem.at[1, half, d], right).wait_recv()

    states_in(0)
    gate_half(0)
    for n in range(4, R + 1):
        for lap in range(2):
            w_arrived(n, lap)
    if NK == 2:
        other = cotg.at[:, lanes_of(1 - k, OT)]
        remote(other, other, cotp_sem.at[0], cotp_sem.at[1], right).wait_recv()

    WIDE = 256

    def up_part(j, carry):
        ls = lanes_of(j, WIDE)
        upp[:, ls] = jnp.dot(cotg[...], wg[:, ls], preferred_element_type=F32).astype(BF16)
        return carry

    lax.fori_loop(0, C // WIDE, up_part, 0)

    def up_copy(d):
        to = plus(y, d, NY)
        return remote(upp.at[rows_of(to), :], up_in.at[d], up_sem.at[0, d], up_sem.at[1, d], dev(to, z))

    for d in range(1, NY):
        up_copy(d).start()

    gate_half(1)

    over_rows = (((0,), (0,)), ((), ()))

    def gw_part(half):
        def body(i, carry):
            block = lax.rem(z + R + NZ - i, NZ)
            gwp[block, :, pl.ds(half * HC, HC)] = lax.dot_general(
                cotg[:, lanes_of(block)], gg[:, pl.ds(half * HC, HC)], over_rows, preferred_element_type=F32
            ).astype(BF16)
            return carry

        lax.fori_loop(0, NZ, body, 0)

    def gw_block(direction, half, step):
        far = long_way(direction, half) - step
        return plus(z, far if direction == 0 else -far, NZ)

    def gw_copy(direction, half, step, part):
        sem, into = (gwr_sem, gw_r) if direction == 0 else (gwl_sem, gw_l)
        rows = pl.ds(part * HALF, HALF)
        return remote(
            gwp.at[gw_block(direction, half, step), rows, pl.ds(half * HC, HC)],
            into.at[half, step, rows, :],
            sem.at[0, half, step, part],
            sem.at[1, half, step, part],
            right if direction == 0 else left,
        )

    def gw_arrived(step, half):
        cols = pl.ds(half * HC, HC)
        for part in range(2):
            rows = pl.ds(part * HALF, HALF)
            for direction in range(2):
                steps = long_way(direction, half)
                if step <= steps:
                    gw_copy(direction, half, step - 1, part).wait_recv()
                if step < steps:
                    at = gw_block(direction, half, step)
                    came = gw_r if direction == 0 else gw_l
                    mine = gwp[at, rows, cols].astype(F32)
                    gwp[at, rows, cols] = (mine + came[half, step - 1, rows, :].astype(F32)).astype(BF16)
                    gw_copy(direction, half, step, part).start()

    def gw_start(half):
        g_arrived(half)
        gw_part(half)
        for direction in range(2):
            if long_way(direction, half) > 0:
                for part in range(2):
                    gw_copy(direction, half, 0, part).start()

    def out_part(j, carry):
        ls = lanes_of(j, WIDE)
        outp[:, ls] = lax.dot_general(gg[...], wg[ls, :], turned, preferred_element_type=F32).astype(BF16)
        return carry


    def pair_copy():
        return remote(
            outp.at[:, lanes_of(1 - k, OT)], pair_in, pair_sem.at[0], pair_sem.at[1], dev(y, z, x, 1 - k)
        )

    def outy_copy(d):
        to = plus(y, d, NY)
        return remote(outh.at[rows_of(to), :], out_y.at[y], outy_sem.at[0, d], outy_sem.at[1, d], dev(to, z))

    def outx_copy(d):
        to = plus(x, d, NX)
        return remote(out_y.at[to], out_x.at[x], outx_sem.at[0, d], outx_sem.at[1, d], dev(y, z, to))

    def out_over_y():
        if NK == 2:
            pair_copy().wait_recv()
            outh[...] = (outp[:, lanes_of(k, OT)].astype(F32) + pair_in[...].astype(F32)).astype(BF16)
        else:
            outh[...] = outp[...]
        for d in range(1, NY):
            outy_copy(d).start()
        out_y[y] = outh[rows_of(y), :]

    def out_over_x():
        for d in range(1, NY):
            block = out_y.at[plus(y, -d, NY)]
            remote(block, block, outy_sem.at[0, d], outy_sem.at[1, d], right).wait_recv()
        for d in range(1, NX):
            outx_copy(d).start()
        out_x[x] = out_y[x]

    def out_done():
        for d in range(1, NX):
            block = out_x.at[plus(x, -d, NX)]
            remote(block, block, outx_sem.at[0, d], outx_sem.at[1, d], right).wait_recv()
        value = out_x[0].astype(F32)
        for n in range(1, NX):
            value = value + out_x[n].astype(F32)
        out_ref[...] = value.astype(BF16)

    gw_start(0)
    gw_arrived(1, 0)

    for d in range(1, NY):
        up_copy(d).wait_recv()

    def grad_field(j, carry):
        ls = lanes_of(j)
        up = upp[rows_of(y), ls].astype(F32)
        for d in range(1, NY):
            up = up + up_in[d, :, ls].astype(F32)
        gf = up * sm[0, :, ls]
        gsp[0, pl.ds(0, ROWS), ls] = up * field[:, ls]
        gm[:, ls] = skip_ref[:, ls] * gf
        sml[pl.ds(24 + j, 1), :] = jnp.sum(gf * mixed[:, ls].astype(F32), axis=0, keepdims=True)
        value = gf.astype(BF16)
        gfb[:, ls] = value
        st_out[1, j] = state_of(inb[j], value)
        return carry

    lax.fori_loop(0, NZ, grad_field, 0)
    states_out(1)

    def local_grad(j, carry):
        ls = lanes_of(j)
        gm[:, ls] = gm[:, ls] + jnp.dot(
            tb[j], spread_groups(gfb[:, ls].astype(F32)), preferred_element_type=F32
        )
        return carry

    def tap_grad(i, j):
        ls = lanes_of(j)
        value = gsp[i, pl.ds(0, ROWS), ls]
        for n in range(TAPS):
            tapsum[pl.ds(i * TAPS + n, 1), ls] = jnp.sum(
                value * xpad[i, pl.ds(8 - n, ROWS), ls], axis=0, keepdims=True
            )

    gw_arrived(2, 0)
    lax.fori_loop(0, NZ, local_grad, 0)
    gw_start(1)
    states_row(1)
    lax.fori_loop(0, OY // WIDE, out_part, 0)
    if NK == 2:
        pair_copy().start()
    gw_arrived(3, 0)
    states_back(1)
    gw_arrived(1, 1)
    for n in range(4, R + 1):
        gw_arrived(n, 0)

    def first_taps(j, carry):
        tap_grad(0, j)
        return carry

    lax.fori_loop(0, NZ, first_taps, 0)
    out_over_y()
    states_in(1)

    def grad_mixed(j, carry):
        ls = lanes_of(j)
        value = gm[:, ls] + from_state(entb[j], bef[1, j])
        gsp[1, pl.ds(0, ROWS), ls] = value * sm[2, :, ls]
        gsp[2, pl.ds(0, ROWS), ls] = value * sm[1, :, ls]
        return carry

    lax.fori_loop(0, NZ, grad_mixed, 0)

    grim_copy = remote(
        gsp.at[:, pl.ds(0, 8), :],
        gsp.at[:, pl.ds(ROWS, 8), :],
        grim_sem.at[0],
        grim_sem.at[1],
        (lax.rem(c + last, last + 1), p),
    )

    @pl.when(c > 0)
    def _():
        grim_copy.start()

    def other_taps(j, carry):
        tap_grad(1, j)
        tap_grad(2, j)
        return carry

    gw_arrived(2, 1)
    lax.fori_loop(0, NZ, other_taps, 0)
    tapsum[pl.ds(3 * TAPS, 3), :] = jnp.zeros((3, C), F32)
    gather_groups = (lax.div(iota((C, LANES), 0), MEMBERS) == iota((C, LANES), 1)).astype(F32)
    sml[pl.ds(0, 24), :] = jnp.dot(
        tapsum[...], gather_groups, precision=HIGHEST, preferred_element_type=F32
    )

    def small_z(d):
        return remote(sml, smz.at[d], smz_sem.at[0, d], smz_sem.at[1, d], dev(y, plus(z, d, NZ)))

    def small_y(d):
        return remote(smy.at[0], smy.at[d], smy_sem.at[0, d], smy_sem.at[1, d], dev(plus(y, d, NY), z))

    for d in range(1, NZ):
        small_z(d).start()

    @pl.when(c == last)
    def _():
        gsp[:, pl.ds(ROWS, 8), :] = jnp.zeros((3, 8, C), F32)

    @pl.when(c < last)
    def _():
        grim_copy.wait_recv()

    def streams_grad(j, carry):
        ls = lanes_of(j)
        for i in range(3):
            total = taps[i, pl.ds(0, 1), ls] * gsp[i, pl.ds(0, ROWS), ls]
            for n in range(1, TAPS):
                total = total + taps[i, pl.ds(n, 1), ls] * gsp[i, pl.ds(n, ROWS), ls]
            gs_ref[i, :, ls] = total.astype(BF16)
        return carry

    out_over_x()
    gw_arrived(3, 1)
    lax.fori_loop(0, NZ, streams_grad, 0)

    total = sml[...]
    for d in range(1, NZ):
        small_z(d).wait_recv()
        total = total + smz[d]
    smy[0] = total
    for d in range(1, NY):
        small_y(d).start()

    out_done()
    for n in range(4, R + 1):
        gw_arrived(n, 1)
    for half in range(2):
        cols = pl.ds(half * HC, HC)
        mine = gwp[z, :, cols].astype(F32)
        for direction, came in ((0, gw_r), (1, gw_l)):
            if long_way(direction, half) > 0:
                mine = mine + came[half, long_way(direction, half) - 1].astype(F32)
        gw_ref[:, cols] = mine

    total = smy[0]
    for d in range(1, NY):
        small_y(d).wait_recv()
        total = total + smy[d]
    for i in range(3):
        gshort_ref[i] = total[i * TAPS : (i + 1) * TAPS, :G]
    for j in range(NZ):
        gskip_ref[:, pl.ds(j * LANES, LANES)] = total[24 + j : 25 + j, :]

    @pl.when(c < last)
    def _():
        rim_copy.wait_send()

    @pl.when(c > 0)
    def _():
        grim_copy.wait_send()

    for direction in range(2):
        for half in range(2):
            for step in range(long_way(direction, half)):
                w_copy(direction, half, step).wait_send()
                gw_copy(direction, half, step, 0).wait_send()
                gw_copy(direction, half, step, 1).wait_send()
    for d in range(NX):
        unless_self(d, lambda: cot_copy(d).wait_send())
    if NK == 2:
        cot_pair().wait_send()
        pair_copy().wait_send()
    for d in range(1, NX):
        outx_copy(d).wait_send()
    for d in range(1, NY):
        outy_copy(d).wait_send()
    for d in range(1, NY):
        g_copy(d, 0).wait_send()
        g_copy(d, 1).wait_send()
        up_copy(d).wait_send()
        small_y(d).wait_send()
        for way in range(2):
            remote(tot.at[way, y], tot.at[way, y], tot_sem.at[way, 0, d], tot_sem.at[way, 1, d], right).wait_send()
    for d in range(1, NZ):
        small_z(d).wait_send()
        for way in range(2):
            for buf, sem in ((st_out, stz_sem), (ret_out, bef_sem)):
                block = buf.at[way, plus(z, d, NZ)]
                remote(block, block, sem.at[way, 0, d], sem.at[way, 1, d], right).wait_send()


def hand_over(*refs):
    ins, outs, held, sem = refs[:5], refs[5:10], refs[10:15], refs[15]
    loads = [pltpu.make_async_copy(ins[i], held[i], sem.at[0, i]) for i in range(5)]
    stores = [pltpu.make_async_copy(held[i], outs[i], sem.at[1, i]) for i in range(5)]
    order = (4, 1, 0, 2, 3)
    for i in order:
        loads[i].start()
    for i in order:
        loads[i].wait()
        stores[i].start()
    for i in order:
        stores[i].wait()


def shards(dims, streams, short_filter, residues, rates, skip, out_weight, out_cotangent):
    NX, NY, NZ, NK = dims
    C = streams.shape[2]
    G = residues.shape[1]
    OT = out_cotangent.shape[1]
    OY = NZ * ROWS
    R = NZ // 2
    vmem = pltpu.VMEM
    dma = pltpu.SemaphoreType.DMA
    whole = pl.BlockSpec(memory_space=pltpu.VMEM)
    scratch = [
        vmem((3, ROWS + 8, C), F32),
        vmem((3, 16, C), BF16),
        vmem((3, ROWS, C), F32),
        vmem((ROWS, C), BF16),
        vmem((ROWS, C), F32),
        vmem((ROWS, C), BF16),
        vmem((ROWS, C), F32),
        vmem((NZ, ROWS, PER_TILE * LANES), BF16),
        vmem((NZ, ROWS, PER_TILE * LANES), BF16),
        vmem((NZ, 2 * ROWS, LANES), BF16),
        vmem((NZ, 2 * ROWS, LANES), BF16),
        vmem((NZ, ROWS, 3 * LANES), BF16),
        vmem((NZ, ROWS, 3 * LANES), BF16),
        vmem((MODES, C), F32),
        vmem((MODES, C), F32),
        vmem((8, C), F32),
        vmem((3, 8, C), F32),
        vmem((2, G, LANES), F32),
        vmem((2, NZ, MODES, LANES), F32),
        vmem((2, NZ, MODES, LANES), F32),
        vmem((2, NY, MODES, LANES), F32),
        vmem((2, NZ, MODES, LANES), F32),
        vmem((2, NZ, MODES, LANES), F32),
        vmem((OY, C), BF16),
        vmem((NY * ROWS, OY), BF16),
        vmem((NY * ROWS, C), BF16),
        vmem((NY * ROWS, C), BF16),
        vmem((NY, ROWS, C), BF16),
        vmem((NY * ROWS, OY), BF16),
        vmem((NY * ROWS, OT), BF16),
        vmem((NY * ROWS, OT), BF16),
        vmem((NY, ROWS, OT), BF16),
        vmem((NX, ROWS, OT), BF16),
        vmem((NZ, ROWS, C), BF16),
        vmem((2, R, ROWS, C // 2), BF16),
        vmem((2, R, ROWS, C // 2), BF16),
        vmem((3, ROWS + 8, C), F32),
        vmem((24, C), F32),
        vmem((32, LANES), F32),
        vmem((NZ, 32, LANES), F32),
        vmem((NY, 32, LANES), F32),
        dma((2,)),
        dma((NX,)),
        dma((NY,)),
        dma((2,)),
        dma((2, 2, R)),
        dma((2, 2, R)),
        dma((2, 2, NZ)),
        dma((2, 2, NY)),
        dma((2, 2, NZ)),
        dma((2, 2, NY)),
        dma((2, NY)),
        dma((2,)),
        dma((2, NY)),
        dma((2, NX)),
        dma((2, 2, R, 2)),
        dma((2, 2, R, 2)),
        dma((2,)),
        dma((2, NZ)),
        dma((2, NY)),
    ]
    output, grad_streams, grad_short, grad_skip, grad_weight = pl.pallas_call(
        functools.partial(kernel, dims),
        out_shape=(
            jax.ShapeDtypeStruct((ROWS, OT), BF16),
            jax.ShapeDtypeStruct(streams.shape, BF16),
            jax.ShapeDtypeStruct(short_filter.shape, F32),
            jax.ShapeDtypeStruct((1, C), F32),
            jax.ShapeDtypeStruct((ROWS, C), F32),
        ),
        in_specs=[whole] * 7,
        out_specs=(whole,) * 5,
        scratch_shapes=scratch,
        compiler_params=pltpu.CompilerParams(
            collective_id=0, has_side_effects=True, vmem_limit_bytes=56 * 1024 * 1024
        ),
        name="mixer",
    )(streams, short_filter, residues, rates, skip.reshape(1, C), out_weight, out_cotangent)
    results = (output, grad_streams, grad_short, grad_skip, grad_weight)
    output, grad_streams, grad_short, grad_skip, grad_weight = pl.pallas_call(
        hand_over,
        out_shape=tuple(jax.ShapeDtypeStruct(a.shape, a.dtype) for a in results),
        in_specs=[pl.BlockSpec(memory_space=pl.ANY)] * 5,
        out_specs=(pl.BlockSpec(memory_space=pl.ANY),) * 5,
        scratch_shapes=[vmem(a.shape, a.dtype) for a in results] + [dma((2, 5))],
        name="hand_over",
    )(*results)
    return output, grad_streams, grad_short, grad_skip.reshape(C), grad_weight


def build(mesh, dims):
    return jax.shard_map(
        functools.partial(shards, dims),
        mesh=mesh,
        in_specs=(
            P(None, "ctx", "tp"),
            P(None, None, "tp"),
            P(None, "tp"),
            P(None, "tp"),
            P("tp"),
            P("ctx", "tp"),
            P("ctx", "tp"),
        ),
        out_specs=(
            P("ctx", "tp"),
            P(None, "ctx", "tp"),
            P(None, None, "tp"),
            P("tp"),
            P("ctx", "tp"),
        ),
        check_vma=False,
    )


def solution(mesh):
    return build(mesh, (4, 4, 8, 2))
```
